32 devices in a mesh: groups: 2 (over x), ctx: 16 (over z, y, core).
Axes of the slice: x: 2, y: 2, z: 4, core: 2. Of those that a mesh axis runs over, the one named last changes fastest.
Arguments:
- value_stream: bfloat16 [4096, 2048], P(('groups', 'ctx')), parts along dimension 0, may hold values from -6 to 6
- gate_stream: bfloat16 [4096, 2048], P(('groups', 'ctx')), parts along dimension 0, may hold values from -6 to 6
- filter_spectrum: bfloat16 [2, 2, 2048, 2048], P(None, None, 'ctx'), may hold values from -6 to 6
- router: bfloat16 [2048, 16], replicated, may hold values from -0.125 to 0.125
- w_gate: bfloat16 [2048, 45056], P(None, 'ctx'), may hold values from -0.125 to 0.125
- w_up: bfloat16 [2048, 45056], P(None, 'ctx'), may hold values from -0.125 to 0.125
- w_down: bfloat16 [45056, 2048], P('ctx'), may hold values from -0.109375 to 0.109375
- route_ids: int32 [2, 4096], P(None, ('groups', 'ctx')), parts along dimension 1, may hold values from 0 to 15, as said below
- route_slots: int32 [2, 4096], P(None, ('groups', 'ctx')), parts along dimension 1, may hold values from 0 to 20, as said below
Outputs:
- layer_out: bfloat16 [4096, 2048], P(('groups', 'ctx')), parts along dimension 0
The draws below stay inside these ranges and needn't reach their ends.
There are 2 independent parts, one for each index of `groups`. The reference program is written for one: setup_inputs(seed, part) draws one part's arguments, and reference() takes and returns one part's arrays. A program takes and returns all parts, laid end to end along the dimension named above; an argument that names none is the same for every part. Nothing has to cross between parts.
Inputs may be any that keep to these rules, and one draw needn't show every extreme that they name: `route_ids`: each token names 2 different experts. route_slots[k, r] is the number of earlier choices of the same expert among the tokens of r's ctx index, tokens taken in order and a token's choices in order k = 0, 1, clipped to 20; so at most 20 choices of one expert from one ctx index are kept, and in every draw some expert has its 20 slots filled from every ctx index.
All inputs are finite; a program needn't handle non-finite values.
Results may differ from the reference program's by a relative error of at most 0.0058.
Values may be sent and summed in bfloat16 or wider, within the bound.
A program may use at most 128 MiB of HBM per device.

```python
import jax
import jax.numpy as jnp
import numpy as np
from jax import lax

D = 2048
FF = 2816
EXPERTS = 16
TOP = 2
TOK_DEV = 128
LENGTH = 2048
CAP = 20
N_CTX = 16


def permute_rows(key_one):
    return jax.random.permutation(key_one, TOK_DEV)


def route_table(key):
    rows_total = TOK_DEV * N_CTX
    key_base, key_popular, key_hot, key_perm = jax.random.split(key, 4)
    base_score = jax.random.randint(key_base, (rows_total, EXPERTS), 0, 64)
    popular = jax.random.randint(key_popular, (EXPERTS,), 0, 48)
    hot_expert = jax.random.randint(key_hot, (), 0, EXPERTS)
    row_ranks = jax.vmap(permute_rows)(jax.random.split(key_perm, N_CTX)).reshape(rows_total)
    expert_range = jnp.arange(EXPERTS, dtype=jnp.int32)
    hot_mask = (row_ranks < 2 * CAP)[:, None] & (expert_range[None, :] == hot_expert)
    scores = (base_score + popular[None, :] + 1000 * hot_mask.astype(jnp.int32)) * EXPERTS + expert_range[None, :]
    top_scores, chosen = lax.top_k(scores, TOP)
    chosen = chosen.astype(jnp.int32)
    onehot = (chosen[:, :, None] == expert_range[None, None, :]).astype(jnp.int32).reshape(N_CTX, TOK_DEV * TOP, EXPERTS)
    running = jnp.cumsum(onehot, axis=1) - onehot
    slot_rank = jnp.sum(running * onehot, axis=2).reshape(rows_total, TOP)
    slot_rank = jnp.minimum(slot_rank, CAP)
    return (chosen.T, slot_rank.T)


def draw_route_ids(key, part):
    return route_table(jax.random.fold_in(key, 11))[0].astype(jnp.int32)


def draw_route_slots(key, part):
    return route_table(jax.random.fold_in(key, 11))[1].astype(jnp.int32)


def shard_levels(rng, extent, pieces, low, largest):
    factor_of, own = 1.0, jax.random.fold_in(rng, 6)
    for dim, parts in pieces:
        draws = jnp.exp(jax.random.uniform(jax.random.fold_in(own, dim), (parts,), jnp.float32, low / len(pieces), largest / len(pieces)))
        factor_of = factor_of * jnp.repeat(draws, extent[dim] // parts).reshape([-1 if axis == dim else 1 for axis in range(len(extent))])
    return factor_of


def normal_values(own_key, extent, width, bound, pieces=(), held_as=jnp.bfloat16):
    gain = shard_levels(own_key, extent, pieces, -0.22, 0.18) if pieces else 1.0
    result = jax.random.normal(own_key, extent, jnp.float32) * width * gain
    return jnp.minimum(jnp.maximum(result, -bound), bound).astype(held_as)


def setup_inputs(seed: int = 0, part: int = 0) -> dict:
    key_of = jax.random.split(jax.random.key(seed), 10)
    part_splits = jax.random.split(jax.random.fold_in(key_of[9], part), 10)
    return {
        "value_stream": normal_values(part_splits[0], (LENGTH, D), 1.0, 6.0, ((0, 16),)),
        "gate_stream": normal_values(part_splits[1], (LENGTH, D), 1.0, 6.0, ((0, 16),)),
        "filter_spectrum": normal_values(key_of[2], (2, 2, LENGTH, D), 1.0, 6.0, ((2, 16),)),
        "router": normal_values(key_of[3], (D, EXPERTS), D ** -0.5, 0.125),
        "w_gate": normal_values(key_of[4], (D, EXPERTS * FF), D ** -0.5, 0.125, ((1, 16),)),
        "w_up": normal_values(key_of[5], (D, EXPERTS * FF), D ** -0.5, 0.125, ((1, 16),)),
        "w_down": normal_values(key_of[6], (EXPERTS * FF, D), FF ** -0.5, 0.109375, ((0, 16),)),
        "route_ids": draw_route_ids(jax.random.fold_in(jax.random.fold_in(key_of[9], part), 71), part),
        "route_slots": draw_route_slots(jax.random.fold_in(jax.random.fold_in(key_of[9], part), 71), part),
    }


def reverse_bits(length_n):
    bit_count = length_n.bit_length() - 1
    positions = np.arange(length_n)
    reversed_index = np.zeros(length_n, dtype=np.int64)
    for position in range(bit_count):
        reversed_index = reversed_index | (positions >> position & 1) << bit_count - 1 - position
    return reversed_index

def reference(value_stream, gate_stream, filter_spectrum, router, w_gate, w_up, w_down, route_ids, route_slots):
    bit_order = reverse_bits(LENGTH)
    natural = np.arange(2 * LENGTH)
    parity = natural % 2
    index_n = bit_order[natural // 2]
    filter_real = filter_spectrum[0][parity, index_n].astype(jnp.float32)
    filter_imag = filter_spectrum[1][parity, index_n].astype(jnp.float32)
    inputs = value_stream.astype(jnp.float32)
    padded = jnp.concatenate([inputs, jnp.zeros_like(inputs)], axis=0)
    spectrum = jnp.fft.fft(padded, axis=0)
    product = spectrum * (filter_real + 1j * filter_imag)
    long_conv = jnp.real(jnp.fft.ifft(product, axis=0))[:LENGTH]
    hyena_out = (gate_stream.astype(jnp.float32) * long_conv).astype(jnp.bfloat16)
    hyena32 = hyena_out.astype(jnp.float32)
    inv_rms = lax.rsqrt(lax.optimization_barrier(jnp.mean(hyena32 * hyena32, axis=1, keepdims=True)) + 1e-06)
    normed = (hyena32 * inv_rms).astype(jnp.bfloat16)
    logits = jnp.dot(normed, router, preferred_element_type=jnp.float32)
    device_of = (jnp.arange(LENGTH) // TOK_DEV).astype(jnp.int32)
    slot_total = N_CTX * EXPERTS * CAP
    buffer = jnp.zeros((slot_total + 1, D), jnp.bfloat16)
    for pick_index in range(TOP):
        expert_ids = route_ids[pick_index].astype(jnp.int32)
        slot_ids = route_slots[pick_index].astype(jnp.int32)
        target = jnp.where(slot_ids < CAP, (device_of * EXPERTS + expert_ids) * CAP + slot_ids, slot_total).astype(jnp.int32)
        buffer = buffer.at[target].set(normed)
    buffer = buffer[:slot_total].reshape(N_CTX, EXPERTS, CAP, D)
    owner_split = N_CTX // EXPERTS
    group_size = FF // owner_split
    gate_stack = w_gate.reshape(D, EXPERTS, FF).transpose(1, 0, 2)
    up_stack = w_up.reshape(D, EXPERTS, FF).transpose(1, 0, 2)
    down_stack = w_down.reshape(EXPERTS, FF, D)

    def one_expert(operands):
        slot_rows, gate_weight, up_weight, down_weight = operands
        flat_rows = slot_rows.reshape(N_CTX * CAP, D)
        gate_part = jnp.dot(flat_rows, gate_weight, preferred_element_type=jnp.float32)
        up_part = jnp.dot(flat_rows, up_weight, preferred_element_type=jnp.float32)
        hidden = (jax.nn.silu(gate_part) * up_part).astype(jnp.bfloat16)
        partial_value = jnp.einsum('rsf,sfd->srd', hidden.reshape(N_CTX * CAP, owner_split, group_size).astype(jnp.float32), down_weight.reshape(owner_split, group_size, D).astype(jnp.float32), precision=lax.Precision.HIGHEST).astype(jnp.bfloat16)
        return lax.optimization_barrier(jnp.sum(partial_value.astype(jnp.float32), axis=0))
    expert_out = lax.map(one_expert, (buffer.transpose(1, 0, 2, 3), gate_stack, up_stack, down_stack))
    expert_out = expert_out.reshape(EXPERTS, N_CTX, CAP, D)
    total_sum = hyena32
    for pick_index in range(TOP):
        expert_ids = route_ids[pick_index].astype(jnp.int32)
        slot_ids = route_slots[pick_index].astype(jnp.int32)
        kept_mask = slot_ids < CAP
        safe_slot = jnp.minimum(slot_ids, CAP - 1).astype(jnp.int32)
        picked = expert_out[expert_ids, device_of, safe_slot]
        gate_value = jax.nn.sigmoid(jnp.take_along_axis(logits, expert_ids[:, None], axis=1)[:, 0])
        total_sum = total_sum + jnp.where(kept_mask[:, None], gate_value[:, None] * picked, 0.0)
    return total_sum.astype(jnp.bfloat16)
```

```python
import jax
import jax.numpy as jnp
import numpy as np
from jax import lax
from jax.experimental import pallas as pl
from jax.experimental.pallas import tpu as pltpu
from jax.sharding import PartitionSpec as P

CAP = 20


two_pi = 2.0 * np.pi
highest = lax.Precision.HIGHEST


def reverse_bits(length_n):
    bit_count = length_n.bit_length() - 1
    positions = np.arange(length_n)
    reversed_index = np.zeros(length_n, dtype=np.int64)
    for position in range(bit_count):
        reversed_index = reversed_index | (positions >> position & 1) << bit_count - 1 - position
    return reversed_index


def spread_table(size_ctx):
    rho = 2 * reverse_bits(size_ctx)[None, :] + np.arange(2)[:, None]
    angle_rad = -two_pi * (np.outer(rho.reshape(-1), np.arange(size_ctx)) % (2 * size_ctx)) / (2 * size_ctx)
    parts = np.stack([np.cos(angle_rad), np.sin(angle_rad)], axis=1)
    return jnp.asarray(parts, jnp.float32)


def fine_table(size_ctx, tok_rows):
    total = 2 * size_ctx * tok_rows
    rho = (2 * reverse_bits(size_ctx)[None, :] + np.arange(2)[:, None]).reshape(-1)
    k = 2 * size_ctx * reverse_bits(tok_rows)[None, :] + rho[:, None]
    step = (k[:, :, None] * np.arange(tok_rows)[None, None, :]) % total
    angle_rad = -two_pi * step / total
    re, im = np.cos(angle_rad), np.sin(angle_rad)
    table = np.stack([np.stack([re, -im], axis=2), np.stack([im, re], axis=2)], axis=1)
    return jnp.asarray(table.reshape(2 * size_ctx, 2 * tok_rows, 2 * tok_rows), jnp.float32)


def convolve(arrived, filter_all, size_ctx, tok_rows, block):
    rho_count = 2 * size_ctx
    coarse = spread_table(size_ctx)
    fine = fine_table(size_ctx, tok_rows)
    samples = arrived.astype(jnp.float32).reshape(size_ctx, tok_rows * block)
    spread = jnp.dot(coarse.reshape(2 * rho_count, size_ctx), samples, precision=highest)
    spread = spread.reshape(rho_count, 2 * tok_rows, block)
    signal = jnp.einsum("rqt,rtc->rqc", fine, spread, precision=highest)
    signal = signal.reshape(rho_count, 2, tok_rows, block)
    filter32 = filter_all.astype(jnp.float32).reshape(2, rho_count, tok_rows, block)
    real_part = signal[:, 0] * filter32[0] - signal[:, 1] * filter32[1]
    imag_part = signal[:, 0] * filter32[1] + signal[:, 1] * filter32[0]
    signal = jnp.concatenate([real_part, imag_part], axis=1)
    spread = jnp.einsum("rqt,rqc->rtc", fine, signal, precision=highest)
    spread = spread.reshape(2 * rho_count, tok_rows * block)
    folded = jnp.dot(coarse.reshape(2 * rho_count, size_ctx).T, spread, precision=highest)
    return (folded / (rho_count * tok_rows)).reshape(size_ctx * tok_rows, block)


def flip_bits(index, mask):
    result = index
    bit = 1
    while bit <= mask:
        if mask & bit:
            result = result + bit * (1 - 2 * ((index // bit) % 2))
        bit *= 2
    return result


COUNT = 16
NEAR = COUNT // 2
HEAD = 16
TAIL = CAP - HEAD
PARTS = HEAD // TAIL


def twist_table(size_ctx, tok_rows):
    rho = (2 * reverse_bits(size_ctx)[:, None] + np.arange(2)[None, :]).reshape(-1)
    angle_rad = -two_pi * np.outer(np.arange(tok_rows), rho) / (2 * size_ctx * tok_rows)
    return jnp.asarray(np.concatenate([np.cos(angle_rad), np.sin(angle_rad)], axis=1), jnp.float32)


def inner_tables(tok_rows):
    angle_rad = -two_pi * (np.outer(reverse_bits(tok_rows), np.arange(tok_rows)) % tok_rows) / tok_rows
    re, im = np.cos(angle_rad), np.sin(angle_rad)
    table = np.block([[re, -im], [im, re]]).astype(np.float32)
    pieces = []
    for matrix in (table, table.T):
        high = matrix.astype(jnp.bfloat16)
        low = (matrix - high.astype(np.float32)).astype(jnp.bfloat16)
        pieces += [high, low]
    return jnp.asarray(np.stack(pieces))


def times_root(pair, power, order):
    power %= order
    re, im = pair
    if power == 0:
        return pair
    if im is None and 4 * power % order:
        cos, sin = float(np.cos(two_pi * power / order)), float(np.sin(two_pi * power / order))
        return (re * cos, re * sin)
    if im is None:
        im = jnp.zeros_like(re)
    if 4 * power == order:
        return (-im, re)
    if 2 * power == order:
        return (-re, -im)
    if 4 * power == 3 * order:
        return (im, -re)
    cos, sin = float(np.cos(two_pi * power / order)), float(np.sin(two_pi * power / order))
    return (re * cos - im * sin, re * sin + im * cos)


def short_transform(values, sign):
    order = len(values)
    if order == 1:
        return values
    even = short_transform(values[0::2], sign)
    odd = short_transform(values[1::2], sign)
    turned = [times_root(odd[i], sign * i, order) for i in range(order // 2)]
    return [(even[i][0] + turned[i][0], even[i][1] + turned[i][1]) for i in range(order // 2)] + [
        (even[i][0] - turned[i][0], even[i][1] - turned[i][1]) for i in range(order // 2)
    ]


VALUES, FILTER, GATE, MIRROR, OWNER, SEND, BACK, ROUTE, PASS = 0, 1, 2, 3, 4, 5, 9, 11, 12
KINDS = 13


def layer_kernel(
    values_hbm, stream_hbm, filter_hbm, tables_hbm, twist_hbm, router_ref, ids_ref, picks_ref, wg_hbm, wu_hbm, wd_hbm,
    out_ref,
    tables_ref, twist_ref, got_values, got_filter, got_gate, wave_high, wave_low, signal, result, blocks,
    own_rows, mirror_rows, normed, mirror_ids, mirror_picks, packed, arrived, rows, hidden, wg, wu, wd,
    done, back, tail_sum, gates, total, own_sem, send_sem, recv_sem, weight_sem,
):
    device = lax.axis_index("ctx")
    group = lax.axis_index("groups")
    tokens, channels = own_rows.shape
    block = channels // COUNT
    half_channels = channels // 2
    part_width = half_channels // PARTS
    hidden_size = wg.shape[1]
    bf16, f32 = jnp.bfloat16, jnp.float32
    peers = [flip_bits(device, mask) for mask in range(COUNT)]
    high_bit = device // NEAR
    far = range(NEAR, COUNT)
    near = range(1, NEAR)

    barrier = pltpu.get_barrier_semaphore()
    for mask in range(1, COUNT):
        pl.semaphore_signal(
            barrier, inc=1, device_id={"ctx": peers[mask]}, device_id_type=pl.DeviceIdType.MESH
        )
    pl.semaphore_signal(
        barrier, inc=1, device_id={"groups": 1 - group}, device_id_type=pl.DeviceIdType.MESH
    )

    def lanes(index):
        return pl.ds(pl.multiple_of(index * block, block), block)

    def remote(kind, mask, src, dst, slot=None):
        slot = mask if slot is None else slot
        return pltpu.make_async_remote_copy(
            src_ref=src,
            dst_ref=dst,
            send_sem=send_sem.at[kind, slot],
            recv_sem=recv_sem.at[kind, slot],
            device_id={"ctx": peers[mask]},
            device_id_type=pl.DeviceIdType.MESH,
        )

    own = [
        pltpu.make_async_copy(values_hbm.at[:, lanes(device)], got_values.at[device], own_sem.at[0]),
        pltpu.make_async_copy(
            filter_hbm.at[:, :, :, lanes(device)], got_filter.at[:, :, device], own_sem.at[1]
        ),
        pltpu.make_async_copy(stream_hbm.at[:, lanes(device)], got_gate.at[device], own_sem.at[2]),
        pltpu.make_async_copy(tables_hbm, tables_ref, own_sem.at[3]),
        pltpu.make_async_copy(twist_hbm, twist_ref, own_sem.at[4]),
    ]
    weights = [
        pltpu.make_async_copy(src, dst, weight_sem.at[i])
        for i, (src, dst) in enumerate(((wg_hbm, wg), (wu_hbm, wu), (wd_hbm, wd)))
    ]
    for copy in own:
        copy.start()

    values_copy, filter_copy, gate_copy, passed = {}, {}, {}, {}
    for mask in range(1, COUNT):
        values_copy[mask] = remote(
            VALUES, mask, values_hbm.at[:, lanes(peers[mask])], got_values.at[device]
        )
        gate_copy[mask] = remote(
            GATE, mask, stream_hbm.at[:, lanes(peers[mask])], got_gate.at[device]
        )
        if mask < NEAR:
            filter_copy[mask] = remote(
                FILTER, mask, filter_hbm.at[:, :, :, lanes(peers[mask])], got_filter.at[:, :, device]
            )
        else:
            filter_copy[mask] = remote(
                FILTER, mask, filter_hbm.at[:, group, :, lanes(peers[mask])], got_filter.at[:, group, device]
            )
            slab = got_filter.at[:, group, peers[mask]]
            passed[mask] = pltpu.make_async_remote_copy(
                src_ref=slab,
                dst_ref=slab,
                send_sem=send_sem.at[PASS, mask],
                recv_sem=recv_sem.at[PASS, mask],
                device_id={"groups": 1 - group},
                device_id_type=pl.DeviceIdType.MESH,
            )
    routes = [
        remote(ROUTE, NEAR, ids_ref, mirror_ids, 0),
        remote(ROUTE, NEAR, picks_ref, mirror_picks, 1),
    ]

    pl.semaphore_wait(barrier, COUNT)
    for mask in far:
        values_copy[mask].start()
        if mask > NEAR:
            values_copy[mask - NEAR].start()
    for copy in routes:
        copy.start()
    for copy in weights:
        copy.start()
    for mask in far:
        values_copy[mask].wait_recv()
        filter_copy[mask].start()
        if mask > NEAR:
            values_copy[mask - NEAR].wait_recv()
            filter_copy[mask - NEAR].start()
    for copy in own:
        copy.wait()

    def reverse(index):
        return int(reverse_bits(COUNT)[index])

    half = tokens
    tile = 16

    @pl.loop(0, tokens // tile)
    def _(step):
        here = pl.ds(pl.multiple_of(step * tile, tile), tile)
        there = pl.ds(pl.multiple_of(half + step * tile, tile), tile)
        samples = [got_values[source, here, :].astype(f32) for source in range(COUNT)]
        zero = jnp.zeros_like(samples[0])
        for parity in range(2):
            pairs = [
                times_root((item, None), -source * parity, 2 * COUNT)
                for source, item in enumerate(samples)
            ]
            pairs = [(re, zero if im is None else im) for re, im in pairs]
            waves = short_transform(pairs, -1)
            for place in range(COUNT):
                re, im = waves[reverse(place)]
                column = 2 * place + parity
                cos = twist_ref[here, column : column + 1]
                sin = twist_ref[here, 2 * COUNT + column : 2 * COUNT + column + 1]
                for span, item in ((here, re * cos - im * sin), (there, re * sin + im * cos)):
                    high = item.astype(bf16)
                    columns = slice(column * block, (column + 1) * block)
                    wave_high[span, columns] = high
                    wave_low[span, columns] = (item - high.astype(f32)).astype(bf16)

    def product(which, columns):
        high, low = wave_high[:, columns], wave_low[:, columns]
        return (
            jnp.dot(tables_ref[which], high, preferred_element_type=f32)
            + jnp.dot(tables_ref[which], low, preferred_element_type=f32)
            + jnp.dot(tables_ref[which + 1], high, preferred_element_type=f32)
        )

    width = 4 * block

    @pl.loop(0, 2 * channels // width)
    def _(step):
        columns = pl.ds(pl.multiple_of(step * width, width), width)
        signal[:, columns] = product(0, columns)

    def filter_places(first, number):
        @pl.loop(first, first + number)
        def _(mask):
            place = 0
            for bit in (1, 2, 4, 8):
                place = place + bit * ((device // bit + mask // bit) % 2)
            for parity in range(2):
                columns = pl.ds(pl.multiple_of((2 * place + parity) * block, block), block)
                re, im = signal[0:half, columns], signal[half : 2 * half, columns]
                filter_re = got_filter[0, parity, place].astype(f32)
                filter_im = got_filter[1, parity, place].astype(f32)
                for span, item in (
                    (slice(0, half), re * filter_re - im * filter_im),
                    (slice(half, 2 * half), re * filter_im + im * filter_re),
                ):
                    high = item.astype(bf16)
                    wave_high[span, columns] = high
                    wave_low[span, columns] = (item - high.astype(f32)).astype(bf16)
            columns = pl.ds(pl.multiple_of(2 * place * block, 2 * block), 2 * block)
            signal[:, columns] = product(2, columns)

    for mask in near:
        gate_copy[mask].start()
    for first in range(0, NEAR, 2):
        for mask in (NEAR + first, NEAR + first + 1):
            filter_copy[mask].wait_recv()
            passed[mask].start()
            gate_copy[mask].start()
        for mask in (first, first + 1):
            if mask:
                filter_copy[mask].wait_recv()
        filter_places(first, 2)
    for first in range(NEAR, COUNT, 2):
        for mask in (first, first + 1):
            passed[mask].wait_recv()
        filter_places(first, 2)

    scale = 1.0 / (2 * COUNT * tokens)

    @pl.loop(0, tokens // tile)
    def _(step):
        here = pl.ds(pl.multiple_of(step * tile, tile), tile)
        there = pl.ds(pl.multiple_of(half + step * tile, tile), tile)
        sums = None
        for parity in range(2):
            waves = [None] * COUNT
            for place in range(COUNT):
                column = 2 * place + parity
                columns = slice(column * block, (column + 1) * block)
                re, im = signal[here, columns], signal[there, columns]
                cos = twist_ref[here, column : column + 1]
                sin = twist_ref[here, 2 * COUNT + column : 2 * COUNT + column + 1]
                waves[reverse(place)] = (re * cos + im * sin, im * cos - re * sin)
            pairs = short_transform(waves, 1)
            parts = [times_root(pair, source * parity, 2 * COUNT)[0] for source, pair in enumerate(pairs)]
            sums = parts if sums is None else [left + right for left, right in zip(sums, parts)]
        for source in range(COUNT):
            result[source, here, :] = sums[source] * scale

    mirror_copy, owner_copy = {}, {}
    for mask in range(1, COUNT):
        mirror_copy[mask] = remote(
            MIRROR, mask, blocks.at[(mask + NEAR) % COUNT], mirror_rows.at[:, lanes(device)]
        )
        owner_copy[mask] = remote(OWNER, mask, blocks.at[mask], own_rows.at[:, lanes(device)])

    def make_block(mask):
        source = peers[mask]
        blocks[mask] = (result[source] * got_gate[source].astype(f32)).astype(bf16)

    for mask in range(NEAR):
        if mask:
            gate_copy[mask].wait_recv()
        make_block(mask)
        mirror_copy[mask + NEAR].start()
    own_rows[:, lanes(device)] = blocks[0]
    for mask in range(NEAR):
        gate_copy[mask + NEAR].wait_recv()
        make_block(mask + NEAR)
        if mask:
            mirror_copy[mask].start()
    mirror_rows[:, lanes(device)] = blocks[NEAR]
    for copy in routes:
        copy.wait()

    near_rows = NEAR * HEAD
    columns_of = [
        pl.ds(pl.multiple_of(base * half_channels, half_channels), half_channels)
        for base in (high_bit, 1 - high_bit)
    ]

    def part_of(chunk, part):
        base = (high_bit, 1 - high_bit)[chunk] * half_channels + part * part_width
        return pl.ds(pl.multiple_of(base, part_width), part_width)

    def targets_of(ids, picks):
        position = jnp.full_like(ids, -1024)
        for mask in range(COUNT):
            position = jnp.where(ids == peers[mask], mask * HEAD, position)
        head = jnp.where(picks < HEAD, position + picks, -1024)
        tail = jnp.where((picks >= HEAD) & (picks < CAP), position + picks - HEAD, -1024)
        return head, tail

    slot_row = lax.broadcasted_iota(jnp.int32, (near_rows, tokens), 0)

    def hits(targets, shift):
        return [slot_row == targets[pick : pick + 1, :] + shift for pick in range(2)]

    def one_hot(targets, shift):
        first, second = hits(targets, shift)
        return jnp.where(first | second, 1.0, 0.0).astype(bf16)

    send_copy = {}
    for kind in range(2):
        for chunk in range(2):
            buffer = 2 * kind + chunk
            for mask in range(NEAR):
                span = pl.ds(mask * HEAD, HEAD)
                src, dst = packed.at[buffer, span], arrived.at[buffer, span]
                if mask:
                    send_copy[buffer, mask] = remote(SEND + buffer, mask, src, dst)
                else:
                    send_copy[buffer, mask] = pltpu.make_async_copy(src, dst, own_sem.at[buffer])

    def dispatch(kind, chunk, source, targets):
        head, tail = targets
        buffer = 2 * kind + chunk
        packed[buffer, :, 0:half_channels] = jnp.dot(
            one_hot(head, 0), source[:, columns_of[chunk]], preferred_element_type=f32
        ).astype(bf16)
        tails = jnp.zeros((near_rows, part_width), f32)
        for part in range(PARTS):
            tails = tails + jnp.dot(
                one_hot(tail, TAIL * part), source[:, part_of(chunk, part)], preferred_element_type=f32
            )
        packed[buffer, :, half_channels:] = tails.astype(bf16)
        for mask in reversed(range(NEAR)):
            send_copy[buffer, mask].start()

    mirror_targets = targets_of(mirror_ids[...], mirror_picks[...])
    for mask in near:
        mirror_copy[mask].wait_recv()
    dispatch(0, 0, mirror_rows, mirror_targets)
    for mask in far:
        mirror_copy[mask].wait_recv()
        owner_copy[mask].start()
    dispatch(0, 1, mirror_rows, mirror_targets)
    for mask in near:
        owner_copy[mask].start()

    tail_rows = NEAR * TAIL
    pick_row = lax.broadcasted_iota(jnp.int32, (tail_rows, near_rows), 0)
    pick_col = lax.broadcasted_iota(jnp.int32, (tail_rows, near_rows), 1)
    pick_base = (pick_row // TAIL) * HEAD + pick_row % TAIL

    def selection(part):
        return jnp.where(pick_col == pick_base + TAIL * part, 1.0, 0.0).astype(bf16)

    back_copy = {}
    for chunk in range(2):
        for mask in range(COUNT):
            kind = 0 if mask >= NEAR else 1
            src = done.at[2 * kind + chunk, pl.ds(mask % NEAR * HEAD, HEAD)]
            dst = back.at[chunk, pl.ds(mask * HEAD, HEAD)]
            if mask:
                back_copy[chunk, mask] = remote(BACK + chunk, mask, src, dst)
            else:
                back_copy[chunk, mask] = pltpu.make_async_copy(src, dst, own_sem.at[4 + chunk])

    def normalise(source, destination, count):
        @pl.loop(0, count // tile)
        def _(step):
            here = pl.ds(pl.multiple_of(step * tile, tile), tile)
            item = source[here, :].astype(f32)
            mean = jnp.sum(item * item, axis=1, keepdims=True) / channels
            destination[here, :] = (item * lax.rsqrt(mean + 1e-06)).astype(bf16)

    def expert(kind):
        for chunk in range(2):
            buffer = 2 * kind + chunk
            for mask in range(NEAR):
                if mask:
                    send_copy[buffer, mask].wait_recv()
                else:
                    send_copy[buffer, mask].wait()
            rows[0:near_rows, columns_of[chunk]] = arrived[buffer, :, 0:half_channels]
            for part in range(PARTS):
                rows[near_rows : near_rows + tail_rows, part_of(chunk, part)] = jnp.dot(
                    selection(part), arrived[buffer, :, half_channels:], preferred_element_type=f32
                ).astype(bf16)
        normalise(rows, rows, near_rows + tail_rows)
        if kind == 0:
            weights[0].wait()
            weights[1].wait()

        @pl.loop(0, hidden_size // 256)
        def _(step):
            columns = pl.ds(pl.multiple_of(step * 256, 256), 256)
            gate_part = jnp.dot(rows[...], wg[:, columns], preferred_element_type=f32)
            up_part = jnp.dot(rows[...], wu[:, columns], preferred_element_type=f32)
            hidden[:, columns] = (jax.nn.silu(gate_part) * up_part).astype(bf16)

        if kind == 0:
            weights[2].wait()
        for chunk in range(2):
            buffer = 2 * kind + chunk
            tail_sum[...] = jnp.zeros_like(tail_sum)

            @pl.loop(0, PARTS)
            def _(part):
                inner = pl.ds(pl.multiple_of(part * part_width, part_width), part_width)
                columns = pl.ds(
                    pl.multiple_of(chunk * half_channels + part * part_width, part_width), part_width
                )
                value = jnp.dot(hidden[...], wd[:, columns], preferred_element_type=f32).astype(bf16)
                done[buffer, :, inner] = value[0:near_rows, :]
                tail_sum[...] += lax.dot_general(
                    selection(part),
                    value[near_rows : near_rows + tail_rows, :],
                    (((0,), (0,)), ((), ())),
                    preferred_element_type=f32,
                )

            done[buffer, :, half_channels:] = tail_sum[...].astype(bf16)
            masks = far if kind == 0 else range(NEAR)
            for mask in masks:
                back_copy[chunk, mask].start()

    own_targets = targets_of(ids_ref[...], picks_ref[...])
    expert(0)
    for mask in near:
        owner_copy[mask].wait_recv()
    dispatch(1, 0, own_rows, own_targets)
    for mask in far:
        owner_copy[mask].wait_recv()
    dispatch(1, 1, own_rows, own_targets)

    normalise(own_rows, normed, tokens)
    logits = lax.dot_general(
        router_ref[...], normed[...], (((1,), (1,)), ((), ())), preferred_element_type=f32
    )
    expert_row = lax.broadcasted_iota(jnp.int32, logits.shape, 0)
    for pick in range(2):
        chosen = jnp.sum(
            jnp.where(expert_row == ids_ref[pick : pick + 1, :], logits, 0.0), axis=0, keepdims=True
        )
        gates[pick : pick + 1, :] = jax.nn.sigmoid(chosen)
    expert(1)

    def weights_of(targets, shift):
        first, second = hits(targets, shift)
        mix = jnp.where(first, gates[0:1, :], 0.0) + jnp.where(second, gates[1:2, :], 0.0)
        high = mix.astype(bf16)
        return high, (mix - high.astype(f32)).astype(bf16)

    def weighted(pair, values):
        dims = (((0,), (0,)), ((), ()))
        return sum(lax.dot_general(piece, values, dims, preferred_element_type=f32) for piece in pair)

    head, tail = own_targets
    for side in range(2):
        shift = -side * near_rows
        span = slice(side * near_rows, (side + 1) * near_rows)
        head_pair = weights_of(head, shift)
        tail_pairs = [weights_of(tail, shift + TAIL * part) for part in range(PARTS)]
        for chunk in range(2):
            for mask in range(side * NEAR, (side + 1) * NEAR):
                if mask:
                    back_copy[chunk, mask].wait_recv()
                else:
                    back_copy[chunk, mask].wait()
            columns = slice(chunk * half_channels, (chunk + 1) * half_channels)
            added = weighted(head_pair, back[chunk, span, 0:half_channels]) + jnp.concatenate(
                [weighted(pair, back[chunk, span, half_channels:]) for pair in tail_pairs], axis=1
            )
            if side == 0:
                total[:, columns] = own_rows[:, columns].astype(f32) + added
            else:
                out_ref[:, columns] = (total[:, columns] + added).astype(bf16)

    for mask in range(1, COUNT):
        values_copy[mask].wait_send()
        filter_copy[mask].wait_send()
        gate_copy[mask].wait_send()
        mirror_copy[mask].wait_send()
        owner_copy[mask].wait_send()
        if mask >= NEAR:
            passed[mask].wait_send()
        for chunk in range(2):
            back_copy[chunk, mask].wait_send()
    for buffer in range(4):
        for mask in near:
            send_copy[buffer, mask].wait_send()


def run_layer(
    value_stream, gate_stream, filter_spectrum, router, w_gate, w_up, w_down, route_ids, route_slots
):
    tokens, channels = value_stream.shape
    hidden_size = w_gate.shape[1]
    block = channels // COUNT
    near_rows = NEAR * HEAD
    half_rows = near_rows + NEAR * TAIL
    part_width = channels // 2 // PARTS
    packed_width = channels // 2 + part_width
    vmem = pl.BlockSpec(memory_space=pltpu.VMEM)
    hbm = pl.BlockSpec(memory_space=pl.ANY)
    bf16, f32, i32 = jnp.bfloat16, jnp.float32, jnp.int32
    return pl.pallas_call(
        layer_kernel,
        out_shape=jax.ShapeDtypeStruct((tokens, channels), bf16),
        in_specs=[hbm] * 5 + [vmem] * 3 + [hbm] * 3,
        out_specs=vmem,
        scratch_shapes=[
            pltpu.VMEM((4, 2 * tokens, 2 * tokens), bf16),
            pltpu.VMEM((tokens, 4 * COUNT), f32),
            pltpu.VMEM((COUNT, tokens, block), bf16),
            pltpu.VMEM((2, 2, COUNT, tokens, block), bf16),
            pltpu.VMEM((COUNT, tokens, block), bf16),
            pltpu.VMEM((2 * tokens, 2 * channels), bf16),
            pltpu.VMEM((2 * tokens, 2 * channels), bf16),
            pltpu.VMEM((2 * tokens, 2 * channels), f32),
            pltpu.VMEM((COUNT, tokens, block), f32),
            pltpu.VMEM((COUNT, tokens, block), bf16),
            pltpu.VMEM((tokens, channels), bf16),
            pltpu.VMEM((tokens, channels), bf16),
            pltpu.VMEM((tokens, channels), bf16),
            pltpu.VMEM((2, tokens), i32),
            pltpu.VMEM((2, tokens), i32),
            pltpu.VMEM((4, near_rows, packed_width), bf16),
            pltpu.VMEM((4, near_rows, packed_width), bf16),
            pltpu.VMEM((half_rows, channels), bf16),
            pltpu.VMEM((half_rows, hidden_size), bf16),
            pltpu.VMEM((channels, hidden_size), bf16),
            pltpu.VMEM((channels, hidden_size), bf16),
            pltpu.VMEM((hidden_size, channels), bf16),
            pltpu.VMEM((4, near_rows, packed_width), bf16),
            pltpu.VMEM((2, 2 * near_rows, packed_width), bf16),
            pltpu.VMEM((near_rows, part_width), f32),
            pltpu.VMEM((8, tokens), f32),
            pltpu.VMEM((tokens, channels), f32),
            pltpu.SemaphoreType.DMA((6,)),
            pltpu.SemaphoreType.DMA((KINDS, COUNT)),
            pltpu.SemaphoreType.DMA((KINDS, COUNT)),
            pltpu.SemaphoreType.DMA((3,)),
        ],
        compiler_params=pltpu.CompilerParams(
            collective_id=1, has_side_effects=True, vmem_limit_bytes=62 * 1024 * 1024
        ),
    )(
        value_stream, gate_stream, filter_spectrum, inner_tables(tokens), twist_table(COUNT, tokens),
        router.T, route_ids, route_slots, w_gate, w_up, w_down,
    )


def local(
    value_stream, gate_stream, filter_spectrum, router, w_gate, w_up, w_down, route_ids, route_slots
):
    tok_rows, channels = value_stream.shape
    size_ctx = lax.axis_size("ctx")
    block = channels // size_ctx
    expert_count = router.shape[1]
    if (
        size_ctx == expert_count == COUNT
        and lax.axis_size("groups") == 2
        and block == tok_rows == 128
        and w_gate.shape[1] % 256 == 0
    ):
        return run_layer(
            value_stream, gate_stream, filter_spectrum, router, w_gate, w_up, w_down, route_ids, route_slots
        )
    arrived = lax.all_to_all(value_stream, "ctx", split_axis=1, concat_axis=0, tiled=True)
    filter_all = lax.all_to_all(filter_spectrum, "ctx", split_axis=3, concat_axis=2, tiled=True)
    long_conv = convolve(arrived, filter_all, size_ctx, tok_rows, block)
    long_conv = lax.all_to_all(
        long_conv.astype(jnp.bfloat16), "ctx", split_axis=0, concat_axis=1, tiled=True
    )
    long_conv = long_conv.astype(jnp.float32)
    hyena_out = (gate_stream.astype(jnp.float32) * long_conv).astype(jnp.bfloat16)
    hyena32 = hyena_out.astype(jnp.float32)
    inv_rms = lax.rsqrt(jnp.mean(hyena32 * hyena32, axis=1, keepdims=True) + 1e-06)
    normed = (hyena32 * inv_rms).astype(jnp.bfloat16)
    logits = jnp.dot(normed, router, preferred_element_type=jnp.float32)
    owner_split = size_ctx // expert_count
    slot_count = expert_count * CAP
    positions = jnp.arange(slot_count, dtype=jnp.int32)
    expert_range = jnp.arange(expert_count, dtype=jnp.int32)
    combine = jnp.zeros((tok_rows, slot_count), jnp.float32)
    dispatch = jnp.zeros((slot_count, channels), jnp.float32)
    for pick_index in range(route_ids.shape[0]):
        expert_ids = route_ids[pick_index]
        slot_ids = route_slots[pick_index]
        target = jnp.where(slot_ids < CAP, expert_ids * CAP + slot_ids, -1)
        slot_hits = target[:, None] == positions[None, :]
        chosen_logit = jnp.sum(
            jnp.where(expert_ids[:, None] == expert_range[None, :], logits, 0.0), axis=1
        )
        gate_value = jax.nn.sigmoid(chosen_logit)
        combine = combine + slot_hits.astype(jnp.float32) * gate_value[:, None]
        dispatch = dispatch + lax.dot_general(
            slot_hits.astype(jnp.bfloat16),
            normed,
            (((0,), (0,)), ((), ())),
            preferred_element_type=jnp.float32,
        )
    buffer = dispatch.astype(jnp.bfloat16).reshape(expert_count, CAP, channels)
    outgoing = jnp.repeat(buffer, owner_split, axis=0)
    slot_rows = lax.all_to_all(outgoing, "ctx", split_axis=0, concat_axis=0, tiled=True)
    flat_rows = slot_rows.reshape(-1, channels)
    gate_part = jnp.dot(flat_rows, w_gate, preferred_element_type=jnp.float32)
    up_part = jnp.dot(flat_rows, w_up, preferred_element_type=jnp.float32)
    hidden = (jax.nn.silu(gate_part) * up_part).astype(jnp.bfloat16)
    partial_value = jnp.dot(hidden, w_down, preferred_element_type=jnp.float32).astype(jnp.bfloat16)
    returned = lax.all_to_all(
        partial_value.reshape(slot_rows.shape), "ctx", split_axis=0, concat_axis=0, tiled=True
    )
    expert_out = jnp.sum(
        returned.astype(jnp.float32).reshape(expert_count, owner_split, CAP, channels), axis=1
    ).reshape(slot_count, channels)
    contribution = jnp.dot(combine, expert_out, precision=highest)
    return (hyena32 + contribution).astype(jnp.bfloat16)


def solution(mesh):
    in_specs = (
        P(("groups", "ctx"), None),
        P(("groups", "ctx"), None),
        P(None, None, "ctx", None),
        P(),
        P(None, "ctx"),
        P(None, "ctx"),
        P("ctx", None),
        P(None, ("groups", "ctx")),
        P(None, ("groups", "ctx")),
    )
    out_specs = P(("groups", "ctx"), None)
    return jax.shard_map(local, mesh=mesh, in_specs=in_specs, out_specs=out_specs, check_vma=False)
```

```python
import jax
import jax.numpy as jnp
import numpy as np
from jax import lax
from jax.experimental import pallas as pl
from jax.experimental.pallas import tpu as pltpu
from jax.sharding import PartitionSpec as P

CAP = 20


two_pi = 2.0 * np.pi
highest = lax.Precision.HIGHEST


def reverse_bits(length_n):
    bit_count = length_n.bit_length() - 1
    positions = np.arange(length_n)
    reversed_index = np.zeros(length_n, dtype=np.int64)
    for position in range(bit_count):
        reversed_index = reversed_index | (positions >> position & 1) << bit_count - 1 - position
    return reversed_index


def spread_table(size_ctx):
    rho = 2 * reverse_bits(size_ctx)[None, :] + np.arange(2)[:, None]
    angle_rad = -two_pi * (np.outer(rho.reshape(-1), np.arange(size_ctx)) % (2 * size_ctx)) / (2 * size_ctx)
    parts = np.stack([np.cos(angle_rad), np.sin(angle_rad)], axis=1)
    return jnp.asarray(parts, jnp.float32)


def fine_table(size_ctx, tok_rows):
    total = 2 * size_ctx * tok_rows
    rho = (2 * reverse_bits(size_ctx)[None, :] + np.arange(2)[:, None]).reshape(-1)
    k = 2 * size_ctx * reverse_bits(tok_rows)[None, :] + rho[:, None]
    step = (k[:, :, None] * np.arange(tok_rows)[None, None, :]) % total
    angle_rad = -two_pi * step / total
    re, im = np.cos(angle_rad), np.sin(angle_rad)
    table = np.stack([np.stack([re, -im], axis=2), np.stack([im, re], axis=2)], axis=1)
    return jnp.asarray(table.reshape(2 * size_ctx, 2 * tok_rows, 2 * tok_rows), jnp.float32)


def convolve(arrived, filter_all, size_ctx, tok_rows, block):
    rho_count = 2 * size_ctx
    coarse = spread_table(size_ctx)
    fine = fine_table(size_ctx, tok_rows)
    samples = arrived.astype(jnp.float32).reshape(size_ctx, tok_rows * block)
    spread = jnp.dot(coarse.reshape(2 * rho_count, size_ctx), samples, precision=highest)
    spread = spread.reshape(rho_count, 2 * tok_rows, block)
    signal = jnp.einsum("rqt,rtc->rqc", fine, spread, precision=highest)
    signal = signal.reshape(rho_count, 2, tok_rows, block)
    filter32 = filter_all.astype(jnp.float32).reshape(2, rho_count, tok_rows, block)
    real_part = signal[:, 0] * filter32[0] - signal[:, 1] * filter32[1]
    imag_part = signal[:, 0] * filter32[1] + signal[:, 1] * filter32[0]
    signal = jnp.concatenate([real_part, imag_part], axis=1)
    spread = jnp.einsum("rqt,rqc->rtc", fine, signal, precision=highest)
    spread = spread.reshape(2 * rho_count, tok_rows * block)
    folded = jnp.dot(coarse.reshape(2 * rho_count, size_ctx).T, spread, precision=highest)
    return (folded / (rho_count * tok_rows)).reshape(size_ctx * tok_rows, block)


def flip_bits(index, mask):
    result = index
    bit = 1
    while bit <= mask:
        if mask & bit:
            result = result + bit * (1 - 2 * ((index // bit) % 2))
        bit *= 2
    return result


COUNT = 16
NEAR = COUNT // 2
HEAD = 16
TAIL = CAP - HEAD
PARTS = HEAD // TAIL


def twist_table(size_ctx, tok_rows):
    rho = (2 * reverse_bits(size_ctx)[:, None] + np.arange(2)[None, :]).reshape(-1)
    angle_rad = -two_pi * np.outer(np.arange(tok_rows), rho) / (2 * size_ctx * tok_rows)
    return jnp.asarray(np.concatenate([np.cos(angle_rad), np.sin(angle_rad)], axis=1), jnp.float32)


def inner_tables(tok_rows):
    angle_rad = -two_pi * (np.outer(reverse_bits(tok_rows), np.arange(tok_rows)) % tok_rows) / tok_rows
    re, im = np.cos(angle_rad), np.sin(angle_rad)
    table = np.block([[re, -im], [im, re]]).astype(np.float32)
    pieces = []
    for matrix in (table, table.T):
        high = matrix.astype(jnp.bfloat16)
        low = (matrix - high.astype(np.float32)).astype(jnp.bfloat16)
        pieces += [high, low]
    return jnp.asarray(np.stack(pieces))


def times_root(pair, power, order):
    power %= order
    re, im = pair
    if power == 0:
        return pair
    if im is None and 4 * power % order:
        cos, sin = float(np.cos(two_pi * power / order)), float(np.sin(two_pi * power / order))
        return (re * cos, re * sin)
    if im is None:
        im = jnp.zeros_like(re)
    if 4 * power == order:
        return (-im, re)
    if 2 * power == order:
        return (-re, -im)
    if 4 * power == 3 * order:
        return (im, -re)
    cos, sin = float(np.cos(two_pi * power / order)), float(np.sin(two_pi * power / order))
    return (re * cos - im * sin, re * sin + im * cos)


def short_transform(values, sign):
    order = len(values)
    if order == 1:
        return values
    even = short_transform(values[0::2], sign)
    odd = short_transform(values[1::2], sign)
    turned = [times_root(odd[i], sign * i, order) for i in range(order // 2)]
    return [(even[i][0] + turned[i][0], even[i][1] + turned[i][1]) for i in range(order // 2)] + [
        (even[i][0] - turned[i][0], even[i][1] - turned[i][1]) for i in range(order // 2)
    ]


VALUES, FILTER, GATE, MIRROR, OWNER, SEND, BACK, ROUTE, PASS = 0, 1, 2, 3, 4, 5, 9, 11, 12
KINDS = 13
WHOLE = 4


def layer_kernel(
    values_hbm, stream_hbm, filter_hbm, tables_hbm, twist_hbm, router_ref, ids_ref, picks_ref, wg_hbm, wu_hbm, wd_hbm,
    out_ref,
    tables_ref, twist_ref, got_values, got_filter, got_gate, wave_high, wave_low, signal, result, blocks,
    own_rows, mirror_rows, normed, mirror_ids, mirror_picks, packed, arrived, rows, hidden, wg, wu, wd,
    done, back, tail_sum, gates, total, own_sem, send_sem, recv_sem, weight_sem,
):
    device = lax.axis_index("ctx")
    group = lax.axis_index("groups")
    tokens, channels = own_rows.shape
    block = channels // COUNT
    half_channels = channels // 2
    part_width = half_channels // PARTS
    hidden_size = wg.shape[1]
    bf16, f32 = jnp.bfloat16, jnp.float32
    peers = [flip_bits(device, mask) for mask in range(COUNT)]
    high_bit = device // NEAR
    far = range(NEAR, COUNT)
    near = range(1, NEAR)

    barrier = pltpu.get_barrier_semaphore()
    for mask in range(1, COUNT):
        pl.semaphore_signal(
            barrier, inc=1, device_id={"ctx": peers[mask]}, device_id_type=pl.DeviceIdType.MESH
        )
    pl.semaphore_signal(
        barrier, inc=1, device_id={"groups": 1 - group}, device_id_type=pl.DeviceIdType.MESH
    )

    def lanes(index):
        return pl.ds(pl.multiple_of(index * block, block), block)

    def remote(kind, mask, src, dst, slot=None):
        slot = mask if slot is None else slot
        return pltpu.make_async_remote_copy(
            src_ref=src,
            dst_ref=dst,
            send_sem=send_sem.at[kind, slot],
            recv_sem=recv_sem.at[kind, slot],
            device_id={"ctx": peers[mask]},
            device_id_type=pl.DeviceIdType.MESH,
        )

    own = [
        pltpu.make_async_copy(values_hbm.at[:, lanes(device)], got_values.at[device], own_sem.at[0]),
        pltpu.make_async_copy(
            filter_hbm.at[:, :, :, lanes(device)], got_filter.at[:, :, device], own_sem.at[1]
        ),
        pltpu.make_async_copy(stream_hbm.at[:, lanes(device)], got_gate.at[device], own_sem.at[2]),
        pltpu.make_async_copy(tables_hbm, tables_ref, own_sem.at[3]),
        pltpu.make_async_copy(twist_hbm, twist_ref, own_sem.at[4]),
    ]
    weights = [
        pltpu.make_async_copy(src, dst, weight_sem.at[i])
        for i, (src, dst) in enumerate(((wg_hbm, wg), (wu_hbm, wu), (wd_hbm, wd)))
    ]
    for copy in own:
        copy.start()

    values_copy, filter_copy, gate_copy, passed = {}, {}, {}, {}
    for mask in range(1, COUNT):
        values_copy[mask] = remote(
            VALUES, mask, values_hbm.at[:, lanes(peers[mask])], got_values.at[device]
        )
        gate_copy[mask] = remote(
            GATE, mask, stream_hbm.at[:, lanes(peers[mask])], got_gate.at[device]
        )
        if mask < WHOLE:
            filter_copy[mask] = remote(
                FILTER, mask, filter_hbm.at[:, :, :, lanes(peers[mask])], got_filter.at[:, :, device]
            )
        else:
            filter_copy[mask] = remote(
                FILTER, mask, filter_hbm.at[:, group, :, lanes(peers[mask])], got_filter.at[:, group, device]
            )
            slab = got_filter.at[:, group, peers[mask]]
            passed[mask] = pltpu.make_async_remote_copy(
                src_ref=slab,
                dst_ref=slab,
                send_sem=send_sem.at[PASS, mask],
                recv_sem=recv_sem.at[PASS, mask],
                device_id={"groups": 1 - group},
                device_id_type=pl.DeviceIdType.MESH,
            )
    routes = [
        remote(ROUTE, NEAR, ids_ref, mirror_ids, 0),
        remote(ROUTE, NEAR, picks_ref, mirror_picks, 1),
    ]

    pl.semaphore_wait(barrier, COUNT)
    for mask in far:
        values_copy[mask].start()
        if mask > NEAR:
            values_copy[mask - NEAR].start()
    early = range(NEAR, NEAR + NEAR // 2)
    late = range(NEAR + NEAR // 2, COUNT)
    for mask in (*early, *near):
        filter_copy[mask].start()
    for copy in routes:
        copy.start()
    for copy in weights:
        copy.start()
    for mask in (*near, *far):
        values_copy[mask].wait_recv()
    for mask in late:
        filter_copy[mask].start()
    for mask in near:
        gate_copy[mask].start()
    for copy in own:
        copy.wait()

    def reverse(index):
        return int(reverse_bits(COUNT)[index])

    half = tokens
    tile = 16

    def spread(step):
        here = pl.ds(pl.multiple_of(step * tile, tile), tile)
        there = pl.ds(pl.multiple_of(half + step * tile, tile), tile)
        samples = [got_values[source, here, :].astype(f32) for source in range(COUNT)]
        zero = jnp.zeros_like(samples[0])
        for parity in range(2):
            pairs = [
                times_root((item, None), -source * parity, 2 * COUNT)
                for source, item in enumerate(samples)
            ]
            pairs = [(re, zero if im is None else im) for re, im in pairs]
            waves = short_transform(pairs, -1)
            for place in range(COUNT):
                re, im = waves[reverse(place)]
                column = 2 * place + parity
                cos = twist_ref[here, column : column + 1]
                sin = twist_ref[here, 2 * COUNT + column : 2 * COUNT + column + 1]
                for span, item in ((here, re * cos - im * sin), (there, re * sin + im * cos)):
                    high = item.astype(bf16)
                    columns = slice(column * block, (column + 1) * block)
                    wave_high[span, columns] = high
                    wave_low[span, columns] = (item - high.astype(f32)).astype(bf16)

    def hand_on(mask):
        filter_copy[mask].wait_recv()
        if mask >= WHOLE:
            passed[mask].start()

    pl.loop(0, tokens // tile // 2)(spread)
    for mask in near:
        hand_on(mask)
    pl.loop(tokens // tile // 2, tokens // tile)(spread)

    def product(which, columns):
        high, low = wave_high[:, columns], wave_low[:, columns]
        return (
            jnp.dot(tables_ref[which], high, preferred_element_type=f32)
            + jnp.dot(tables_ref[which], low, preferred_element_type=f32)
            + jnp.dot(tables_ref[which + 1], high, preferred_element_type=f32)
        )

    width = 4 * block

    @pl.loop(0, 2 * channels // width)
    def _(step):
        columns = pl.ds(pl.multiple_of(step * width, width), width)
        signal[:, columns] = product(0, columns)

    def filter_places(first, number):
        @pl.loop(0, number // 2)
        def _(step):
            columns, highs, lows = [], [], []
            for mask in (first + 2 * step, first + 2 * step + 1):
                place = 0
                for bit in (1, 2, 4, 8):
                    place = place + bit * ((device // bit + mask // bit) % 2)
                columns.append(pl.ds(pl.multiple_of(2 * place * block, 2 * block), 2 * block))
                for parity in range(2):
                    lane = pl.ds(pl.multiple_of((2 * place + parity) * block, block), block)
                    re, im = signal[0:half, lane], signal[half : 2 * half, lane]
                    filter_re = got_filter[0, parity, place].astype(f32)
                    filter_im = got_filter[1, parity, place].astype(f32)
                    item = jnp.concatenate(
                        [re * filter_re - im * filter_im, re * filter_im + im * filter_re], axis=0
                    )
                    high = item.astype(bf16)
                    highs.append(high)
                    lows.append((item - high.astype(f32)).astype(bf16))
            high, low = jnp.concatenate(highs, axis=1), jnp.concatenate(lows, axis=1)
            value = (
                jnp.dot(tables_ref[2], high, preferred_element_type=f32)
                + jnp.dot(tables_ref[2], low, preferred_element_type=f32)
                + jnp.dot(tables_ref[3], high, preferred_element_type=f32)
            )
            for i, column in enumerate(columns):
                signal[:, column] = value[:, 2 * i * block : 2 * (i + 1) * block]

    for mask in early:
        hand_on(mask)
    for mask in near:
        if mask >= WHOLE:
            passed[mask].wait_recv()
    filter_places(0, NEAR)
    for mask in late:
        hand_on(mask)
        gate_copy[mask].start()
        gate_copy[mask - NEAR // 2].start()
    for first in range(NEAR, COUNT, 2):
        for mask in (first, first + 1):
            passed[mask].wait_recv()
        filter_places(first, 2)
    scale = 1.0 / (2 * COUNT * tokens)

    def gather(step):
        here = pl.ds(pl.multiple_of(step * tile, tile), tile)
        there = pl.ds(pl.multiple_of(half + step * tile, tile), tile)
        sums = None
        for parity in range(2):
            waves = [None] * COUNT
            for place in range(COUNT):
                column = 2 * place + parity
                columns = slice(column * block, (column + 1) * block)
                re, im = signal[here, columns], signal[there, columns]
                cos = twist_ref[here, column : column + 1]
                sin = twist_ref[here, 2 * COUNT + column : 2 * COUNT + column + 1]
                waves[reverse(place)] = (re * cos + im * sin, im * cos - re * sin)
            pairs = short_transform(waves, 1)
            parts = [times_root(pair, source * parity, 2 * COUNT)[0] for source, pair in enumerate(pairs)]
            sums = parts if sums is None else [left + right for left, right in zip(sums, parts)]
        for source in range(COUNT):
            result[source, here, :] = sums[source] * scale

    pl.loop(0, tokens // tile)(gather)

    mirror_copy, owner_copy = {}, {}
    for mask in range(1, COUNT):
        mirror_copy[mask] = remote(
            MIRROR, mask, blocks.at[(mask + NEAR) % COUNT], mirror_rows.at[:, lanes(device)]
        )
        owner_copy[mask] = remote(OWNER, mask, blocks.at[mask], own_rows.at[:, lanes(device)])

    def make_block(mask):
        source = peers[mask]
        blocks[mask] = (result[source] * got_gate[source].astype(f32)).astype(bf16)

    for mask in range(NEAR):
        if mask:
            gate_copy[mask].wait_recv()
        make_block(mask)
        mirror_copy[mask + NEAR].start()
        if mask:
            owner_copy[mask].start()
    own_rows[:, lanes(device)] = blocks[0]
    for mask in range(NEAR):
        gate_copy[mask + NEAR].wait_recv()
        make_block(mask + NEAR)
        if mask:
            mirror_copy[mask].start()
    mirror_rows[:, lanes(device)] = blocks[NEAR]
    for copy in routes:
        copy.wait()

    near_rows = NEAR * HEAD
    columns_of = [
        pl.ds(pl.multiple_of(base * half_channels, half_channels), half_channels)
        for base in (high_bit, 1 - high_bit)
    ]

    def part_of(chunk, part):
        base = (high_bit, 1 - high_bit)[chunk] * half_channels + part * part_width
        return pl.ds(pl.multiple_of(base, part_width), part_width)

    def targets_of(ids, picks):
        position = jnp.full_like(ids, -1024)
        for mask in range(COUNT):
            position = jnp.where(ids == peers[mask], mask * HEAD, position)
        head = jnp.where(picks < HEAD, position + picks, -1024)
        tail = jnp.where((picks >= HEAD) & (picks < CAP), position + picks - HEAD, -1024)
        return head, tail

    slot_row = lax.broadcasted_iota(jnp.int32, (near_rows, tokens), 0)

    def hits(targets, shift):
        return [slot_row == targets[pick : pick + 1, :] + shift for pick in range(2)]

    def one_hot(targets, shift):
        first, second = hits(targets, shift)
        return jnp.where(first | second, 1.0, 0.0).astype(bf16)

    send_copy = {}
    for kind in range(2):
        for chunk in range(2):
            buffer = 2 * kind + chunk
            for mask in range(NEAR):
                span = pl.ds(mask * HEAD, HEAD)
                src, dst = packed.at[buffer, span], arrived.at[buffer, span]
                if mask:
                    send_copy[buffer, mask] = remote(SEND + buffer, mask, src, dst)
                else:
                    send_copy[buffer, mask] = pltpu.make_async_copy(src, dst, own_sem.at[buffer])

    def dispatch(kind, chunk, source, targets):
        head, tail = targets
        buffer = 2 * kind + chunk
        packed[buffer, :, 0:half_channels] = jnp.dot(
            one_hot(head, 0), source[:, columns_of[chunk]], preferred_element_type=f32
        ).astype(bf16)
        tails = jnp.zeros((near_rows, part_width), f32)
        for part in range(PARTS):
            tails = tails + jnp.dot(
                one_hot(tail, TAIL * part), source[:, part_of(chunk, part)], preferred_element_type=f32
            )
        packed[buffer, :, half_channels:] = tails.astype(bf16)
        for mask in reversed(range(NEAR)):
            send_copy[buffer, mask].start()

    mirror_targets = targets_of(mirror_ids[...], mirror_picks[...])
    for mask in near:
        mirror_copy[mask].wait_recv()
    dispatch(0, 0, mirror_rows, mirror_targets)
    own_targets = targets_of(ids_ref[...], picks_ref[...])

    def dispatch_near():
        for mask in near:
            owner_copy[mask].wait_recv()
        dispatch(1, 0, own_rows, own_targets)

    def dispatch_far():
        for mask in far:
            owner_copy[mask].wait_recv()
        dispatch(1, 1, own_rows, own_targets)

    for mask in far:
        mirror_copy[mask].wait_recv()
    dispatch(0, 1, mirror_rows, mirror_targets)
    dispatch_near()
    for mask in far:
        owner_copy[mask].start()

    tail_rows = NEAR * TAIL
    pick_row = lax.broadcasted_iota(jnp.int32, (tail_rows, near_rows), 0)
    pick_col = lax.broadcasted_iota(jnp.int32, (tail_rows, near_rows), 1)
    pick_base = (pick_row // TAIL) * HEAD + pick_row % TAIL

    def selection(part):
        return jnp.where(pick_col == pick_base + TAIL * part, 1.0, 0.0).astype(bf16)

    back_copy = {}
    for chunk in range(2):
        for mask in range(COUNT):
            kind = 0 if mask >= NEAR else 1
            src = done.at[2 * kind + chunk, pl.ds(mask % NEAR * HEAD, HEAD)]
            dst = back.at[chunk, pl.ds(mask * HEAD, HEAD)]
            if mask:
                back_copy[chunk, mask] = remote(BACK + chunk, mask, src, dst)
            else:
                back_copy[chunk, mask] = pltpu.make_async_copy(src, dst, own_sem.at[4 + chunk])

    def normalise(source, destination, count):
        @pl.loop(0, count // tile)
        def _(step):
            here = pl.ds(pl.multiple_of(step * tile, tile), tile)
            item = source[here, :].astype(f32)
            mean = jnp.sum(item * item, axis=1, keepdims=True) / channels
            destination[here, :] = (item * lax.rsqrt(mean + 1e-06)).astype(bf16)

    def expert(kind):
        for chunk in range(2):
            buffer = 2 * kind + chunk
            for mask in range(NEAR):
                if mask:
                    send_copy[buffer, mask].wait_recv()
                else:
                    send_copy[buffer, mask].wait()
            rows[0:near_rows, columns_of[chunk]] = arrived[buffer, :, 0:half_channels]
            for part in range(PARTS):
                rows[near_rows : near_rows + tail_rows, part_of(chunk, part)] = jnp.dot(
                    selection(part), arrived[buffer, :, half_channels:], preferred_element_type=f32
                ).astype(bf16)
        if kind == 1:
            for mask in far:
                back_copy[1, mask].start()
        normalise(rows, rows, near_rows + tail_rows)
        if kind == 0:
            weights[0].wait()
            weights[1].wait()

        @pl.loop(0, hidden_size // 256)
        def _(step):
            columns = pl.ds(pl.multiple_of(step * 256, 256), 256)
            gate_part = jnp.dot(rows[...], wg[:, columns], preferred_element_type=f32)
            up_part = jnp.dot(rows[...], wu[:, columns], preferred_element_type=f32)
            hidden[:, columns] = (jax.nn.silu(gate_part) * up_part).astype(bf16)

        if kind == 0:
            weights[2].wait()
            dispatch_far()
        for chunk in range(2):
            buffer = 2 * kind + chunk
            tail_sum[...] = jnp.zeros_like(tail_sum)

            @pl.loop(0, PARTS)
            def _(part):
                inner = pl.ds(pl.multiple_of(part * part_width, part_width), part_width)
                columns = pl.ds(
                    pl.multiple_of(chunk * half_channels + part * part_width, part_width), part_width
                )
                value = jnp.dot(hidden[...], wd[:, columns], preferred_element_type=f32).astype(bf16)
                done[buffer, :, inner] = value[0:near_rows, :]
                tail_sum[...] += lax.dot_general(
                    selection(part),
                    value[near_rows : near_rows + tail_rows, :],
                    (((0,), (0,)), ((), ())),
                    preferred_element_type=f32,
                )

            done[buffer, :, half_channels:] = tail_sum[...].astype(bf16)
            masks = far if kind == 0 else range(NEAR)
            for mask in () if kind == 0 and chunk == 1 else masks:
                back_copy[chunk, mask].start()

    expert(0)
    normalise(own_rows, normed, tokens)
    logits = lax.dot_general(
        router_ref[...], normed[...], (((1,), (1,)), ((), ())), preferred_element_type=f32
    )
    expert_row = lax.broadcasted_iota(jnp.int32, logits.shape, 0)
    for pick in range(2):
        chosen = jnp.sum(
            jnp.where(expert_row == ids_ref[pick : pick + 1, :], logits, 0.0), axis=0, keepdims=True
        )
        gates[pick : pick + 1, :] = jax.nn.sigmoid(chosen)
    expert(1)

    def weights_of(targets, shift):
        first, second = hits(targets, shift)
        mix = jnp.where(first, gates[0:1, :], 0.0) + jnp.where(second, gates[1:2, :], 0.0)
        high = mix.astype(bf16)
        return high, (mix - high.astype(f32)).astype(bf16)

    def weighted(pair, values):
        dims = (((0,), (0,)), ((), ()))
        return sum(lax.dot_general(piece, values, dims, preferred_element_type=f32) for piece in pair)

    head, tail = own_targets
    for side in range(2):
        shift = -side * near_rows
        span = slice(side * near_rows, (side + 1) * near_rows)
        head_pair = weights_of(head, shift)
        tail_pairs = [weights_of(tail, shift + TAIL * part) for part in range(PARTS)]
        for chunk in range(2):
            for mask in range(side * NEAR, (side + 1) * NEAR):
                if mask:
                    back_copy[chunk, mask].wait_recv()
                else:
                    back_copy[chunk, mask].wait()
            columns = slice(chunk * half_channels, (chunk + 1) * half_channels)
            added = weighted(head_pair, back[chunk, span, 0:half_channels]) + jnp.concatenate(
                [weighted(pair, back[chunk, span, half_channels:]) for pair in tail_pairs], axis=1
            )
            if side == 0:
                total[:, columns] = own_rows[:, columns].astype(f32) + added
            else:
                out_ref[:, columns] = (total[:, columns] + added).astype(bf16)

    for mask in range(1, COUNT):
        values_copy[mask].wait_send()
        filter_copy[mask].wait_send()
        gate_copy[mask].wait_send()
        mirror_copy[mask].wait_send()
        owner_copy[mask].wait_send()
        if mask >= WHOLE:
            passed[mask].wait_send()
        for chunk in range(2):
            back_copy[chunk, mask].wait_send()
    for buffer in range(4):
        for mask in near:
            send_copy[buffer, mask].wait_send()


def run_layer(
    value_stream, gate_stream, filter_spectrum, router, w_gate, w_up, w_down, route_ids, route_slots
):
    tokens, channels = value_stream.shape
    hidden_size = w_gate.shape[1]
    block = channels // COUNT
    near_rows = NEAR * HEAD
    half_rows = near_rows + NEAR * TAIL
    part_width = channels // 2 // PARTS
    packed_width = channels // 2 + part_width
    vmem = pl.BlockSpec(memory_space=pltpu.VMEM)
    hbm = pl.BlockSpec(memory_space=pl.ANY)
    bf16, f32, i32 = jnp.bfloat16, jnp.float32, jnp.int32
    return pl.pallas_call(
        layer_kernel,
        out_shape=jax.ShapeDtypeStruct((tokens, channels), bf16),
        in_specs=[hbm] * 5 + [vmem] * 3 + [hbm] * 3,
        out_specs=vmem,
        scratch_shapes=[
            pltpu.VMEM((4, 2 * tokens, 2 * tokens), bf16),
            pltpu.VMEM((tokens, 4 * COUNT), f32),
            pltpu.VMEM((COUNT, tokens, block), bf16),
            pltpu.VMEM((2, 2, COUNT, tokens, block), bf16),
            pltpu.VMEM((COUNT, tokens, block), bf16),
            pltpu.VMEM((2 * tokens, 2 * channels), bf16),
            pltpu.VMEM((2 * tokens, 2 * channels), bf16),
            pltpu.VMEM((2 * tokens, 2 * channels), f32),
            pltpu.VMEM((COUNT, tokens, block), f32),
            pltpu.VMEM((COUNT, tokens, block), bf16),
            pltpu.VMEM((tokens, channels), bf16),
            pltpu.VMEM((tokens, channels), bf16),
            pltpu.VMEM((tokens, channels), bf16),
            pltpu.VMEM((2, tokens), i32),
            pltpu.VMEM((2, tokens), i32),
            pltpu.VMEM((4, near_rows, packed_width), bf16),
            pltpu.VMEM((4, near_rows, packed_width), bf16),
            pltpu.VMEM((half_rows, channels), bf16),
            pltpu.VMEM((half_rows, hidden_size), bf16),
            pltpu.VMEM((channels, hidden_size), bf16),
            pltpu.VMEM((channels, hidden_size), bf16),
            pltpu.VMEM((hidden_size, channels), bf16),
            pltpu.VMEM((4, near_rows, packed_width), bf16),
            pltpu.VMEM((2, 2 * near_rows, packed_width), bf16),
            pltpu.VMEM((near_rows, part_width), f32),
            pltpu.VMEM((8, tokens), f32),
            pltpu.VMEM((tokens, channels), f32),
            pltpu.SemaphoreType.DMA((6,)),
            pltpu.SemaphoreType.DMA((KINDS, COUNT)),
            pltpu.SemaphoreType.DMA((KINDS, COUNT)),
            pltpu.SemaphoreType.DMA((3,)),
        ],
        compiler_params=pltpu.CompilerParams(
            collective_id=1, has_side_effects=True, vmem_limit_bytes=62 * 1024 * 1024
        ),
    )(
        value_stream, gate_stream, filter_spectrum, inner_tables(tokens), twist_table(COUNT, tokens),
        router.T, route_ids, route_slots, w_gate, w_up, w_down,
    )


def local(
    value_stream, gate_stream, filter_spectrum, router, w_gate, w_up, w_down, route_ids, route_slots
):
    tok_rows, channels = value_stream.shape
    size_ctx = lax.axis_size("ctx")
    block = channels // size_ctx
    expert_count = router.shape[1]
    if (
        size_ctx == expert_count == COUNT
        and lax.axis_size("groups") == 2
        and block == tok_rows == 128
        and w_gate.shape[1] % 256 == 0
    ):
        return run_layer(
            value_stream, gate_stream, filter_spectrum, router, w_gate, w_up, w_down, route_ids, route_slots
        )
    arrived = lax.all_to_all(value_stream, "ctx", split_axis=1, concat_axis=0, tiled=True)
    filter_all = lax.all_to_all(filter_spectrum, "ctx", split_axis=3, concat_axis=2, tiled=True)
    long_conv = convolve(arrived, filter_all, size_ctx, tok_rows, block)
    long_conv = lax.all_to_all(
        long_conv.astype(jnp.bfloat16), "ctx", split_axis=0, concat_axis=1, tiled=True
    )
    long_conv = long_conv.astype(jnp.float32)
    hyena_out = (gate_stream.astype(jnp.float32) * long_conv).astype(jnp.bfloat16)
    hyena32 = hyena_out.astype(jnp.float32)
    inv_rms = lax.rsqrt(jnp.mean(hyena32 * hyena32, axis=1, keepdims=True) + 1e-06)
    normed = (hyena32 * inv_rms).astype(jnp.bfloat16)
    logits = jnp.dot(normed, router, preferred_element_type=jnp.float32)
    owner_split = size_ctx // expert_count
    slot_count = expert_count * CAP
    positions = jnp.arange(slot_count, dtype=jnp.int32)
    expert_range = jnp.arange(expert_count, dtype=jnp.int32)
    combine = jnp.zeros((tok_rows, slot_count), jnp.float32)
    dispatch = jnp.zeros((slot_count, channels), jnp.float32)
    for pick_index in range(route_ids.shape[0]):
        expert_ids = route_ids[pick_index]
        slot_ids = route_slots[pick_index]
        target = jnp.where(slot_ids < CAP, expert_ids * CAP + slot_ids, -1)
        slot_hits = target[:, None] == positions[None, :]
        chosen_logit = jnp.sum(
            jnp.where(expert_ids[:, None] == expert_range[None, :], logits, 0.0), axis=1
        )
        gate_value = jax.nn.sigmoid(chosen_logit)
        combine = combine + slot_hits.astype(jnp.float32) * gate_value[:, None]
        dispatch = dispatch + lax.dot_general(
            slot_hits.astype(jnp.bfloat16),
            normed,
            (((0,), (0,)), ((), ())),
            preferred_element_type=jnp.float32,
        )
    buffer = dispatch.astype(jnp.bfloat16).reshape(expert_count, CAP, channels)
    outgoing = jnp.repeat(buffer, owner_split, axis=0)
    slot_rows = lax.all_to_all(outgoing, "ctx", split_axis=0, concat_axis=0, tiled=True)
    flat_rows = slot_rows.reshape(-1, channels)
    gate_part = jnp.dot(flat_rows, w_gate, preferred_element_type=jnp.float32)
    up_part = jnp.dot(flat_rows, w_up, preferred_element_type=jnp.float32)
    hidden = (jax.nn.silu(gate_part) * up_part).astype(jnp.bfloat16)
    partial_value = jnp.dot(hidden, w_down, preferred_element_type=jnp.float32).astype(jnp.bfloat16)
    returned = lax.all_to_all(
        partial_value.reshape(slot_rows.shape), "ctx", split_axis=0, concat_axis=0, tiled=True
    )
    expert_out = jnp.sum(
        returned.astype(jnp.float32).reshape(expert_count, owner_split, CAP, channels), axis=1
    ).reshape(slot_count, channels)
    contribution = jnp.dot(combine, expert_out, precision=highest)
    return (hyena32 + contribution).astype(jnp.bfloat16)


def solution(mesh):
    in_specs = (
        P(("groups", "ctx"), None),
        P(("groups", "ctx"), None),
        P(None, None, "ctx", None),
        P(),
        P(None, "ctx"),
        P(None, "ctx"),
        P("ctx", None),
        P(None, ("groups", "ctx")),
        P(None, ("groups", "ctx")),
    )
    out_specs = P(("groups", "ctx"), None)
    return jax.shard_map(local, mesh=mesh, in_specs=in_specs, out_specs=out_specs, check_vma=False)
```

```python
import jax
import jax.numpy as jnp
import numpy as np
from jax import lax
from jax.experimental import pallas as pl
from jax.experimental.pallas import tpu as pltpu
from jax.sharding import PartitionSpec as P

CAP = 20


two_pi = 2.0 * np.pi
highest = lax.Precision.HIGHEST


def reverse_bits(length_n):
    bit_count = length_n.bit_length() - 1
    positions = np.arange(length_n)
    reversed_index = np.zeros(length_n, dtype=np.int64)
    for position in range(bit_count):
        reversed_index = reversed_index | (positions >> position & 1) << bit_count - 1 - position
    return reversed_index


def spread_table(size_ctx):
    rho = 2 * reverse_bits(size_ctx)[None, :] + np.arange(2)[:, None]
    angle_rad = -two_pi * (np.outer(rho.reshape(-1), np.arange(size_ctx)) % (2 * size_ctx)) / (2 * size_ctx)
    parts = np.stack([np.cos(angle_rad), np.sin(angle_rad)], axis=1)
    return jnp.asarray(parts, jnp.float32)


def fine_table(size_ctx, tok_rows):
    total = 2 * size_ctx * tok_rows
    rho = (2 * reverse_bits(size_ctx)[None, :] + np.arange(2)[:, None]).reshape(-1)
    k = 2 * size_ctx * reverse_bits(tok_rows)[None, :] + rho[:, None]
    step = (k[:, :, None] * np.arange(tok_rows)[None, None, :]) % total
    angle_rad = -two_pi * step / total
    re, im = np.cos(angle_rad), np.sin(angle_rad)
    table = np.stack([np.stack([re, -im], axis=2), np.stack([im, re], axis=2)], axis=1)
    return jnp.asarray(table.reshape(2 * size_ctx, 2 * tok_rows, 2 * tok_rows), jnp.float32)


def convolve(arrived, filter_all, size_ctx, tok_rows, block):
    rho_count = 2 * size_ctx
    coarse = spread_table(size_ctx)
    fine = fine_table(size_ctx, tok_rows)
    samples = arrived.astype(jnp.float32).reshape(size_ctx, tok_rows * block)
    spread = jnp.dot(coarse.reshape(2 * rho_count, size_ctx), samples, precision=highest)
    spread = spread.reshape(rho_count, 2 * tok_rows, block)
    signal = jnp.einsum("rqt,rtc->rqc", fine, spread, precision=highest)
    signal = signal.reshape(rho_count, 2, tok_rows, block)
    filter32 = filter_all.astype(jnp.float32).reshape(2, rho_count, tok_rows, block)
    real_part = signal[:, 0] * filter32[0] - signal[:, 1] * filter32[1]
    imag_part = signal[:, 0] * filter32[1] + signal[:, 1] * filter32[0]
    signal = jnp.concatenate([real_part, imag_part], axis=1)
    spread = jnp.einsum("rqt,rqc->rtc", fine, signal, precision=highest)
    spread = spread.reshape(2 * rho_count, tok_rows * block)
    folded = jnp.dot(coarse.reshape(2 * rho_count, size_ctx).T, spread, precision=highest)
    return (folded / (rho_count * tok_rows)).reshape(size_ctx * tok_rows, block)


def flip_bits(index, mask):
    result = index
    bit = 1
    while bit <= mask:
        if mask & bit:
            result = result + bit * (1 - 2 * ((index // bit) % 2))
        bit *= 2
    return result


COUNT = 16
NEAR = COUNT // 2
HEAD = 16
TAIL = CAP - HEAD
PARTS = HEAD // TAIL


def twist_table(size_ctx, tok_rows):
    rho = (2 * reverse_bits(size_ctx)[:, None] + np.arange(2)[None, :]).reshape(-1)
    angle_rad = -two_pi * np.outer(np.arange(tok_rows), rho) / (2 * size_ctx * tok_rows)
    return jnp.asarray(np.concatenate([np.cos(angle_rad), np.sin(angle_rad)], axis=1), jnp.float32)


def inner_tables(tok_rows):
    angle_rad = -two_pi * (np.outer(reverse_bits(tok_rows), np.arange(tok_rows)) % tok_rows) / tok_rows
    re, im = np.cos(angle_rad), np.sin(angle_rad)
    table = np.block([[re, -im], [im, re]]).astype(np.float32)
    pieces = []
    for matrix in (table, table.T):
        high = matrix.astype(jnp.bfloat16)
        low = (matrix - high.astype(np.float32)).astype(jnp.bfloat16)
        pieces += [high, low]
    return jnp.asarray(np.stack(pieces))


def times_root(pair, power, order):
    power %= order
    re, im = pair
    if power == 0:
        return pair
    if im is None and 4 * power % order:
        cos, sin = float(np.cos(two_pi * power / order)), float(np.sin(two_pi * power / order))
        return (re * cos, re * sin)
    if im is None:
        im = jnp.zeros_like(re)
    if 4 * power == order:
        return (-im, re)
    if 2 * power == order:
        return (-re, -im)
    if 4 * power == 3 * order:
        return (im, -re)
    cos, sin = float(np.cos(two_pi * power / order)), float(np.sin(two_pi * power / order))
    return (re * cos - im * sin, re * sin + im * cos)


def short_transform(values, sign):
    order = len(values)
    if order == 1:
        return values
    even = short_transform(values[0::2], sign)
    odd = short_transform(values[1::2], sign)
    turned = [times_root(odd[i], sign * i, order) for i in range(order // 2)]
    return [(even[i][0] + turned[i][0], even[i][1] + turned[i][1]) for i in range(order // 2)] + [
        (even[i][0] - turned[i][0], even[i][1] - turned[i][1]) for i in range(order // 2)
    ]


VALUES, FILTER, GATE, MIRROR, OWNER, SEND, BACK, ROUTE, PASS = 0, 1, 2, 3, 4, 5, 9, 13, 14
KINDS = 15
BACKS = 4
WHOLE = 4


def layer_kernel(
    values_hbm, stream_hbm, filter_hbm, tables_hbm, twist_hbm, router_ref, ids_ref, picks_ref, wg_hbm, wu_hbm, wd_hbm,
    out_ref,
    tables_ref, twist_ref, got_values, got_filter, got_gate, wave_high, wave_low, signal, result, blocks,
    own_rows, mirror_rows, normed, mirror_ids, mirror_picks, packed, arrived, rows, hidden, wg, wu, wd,
    inverse, gate_sum, up_sum, done, back, tail_sum, gates, total, own_sem, send_sem, recv_sem, weight_sem,
):
    device = lax.axis_index("ctx")
    group = lax.axis_index("groups")
    tokens, channels = own_rows.shape
    block = channels // COUNT
    half_channels = channels // 2
    part_width = half_channels // PARTS
    hidden_size = wg.shape[1]
    bf16, f32 = jnp.bfloat16, jnp.float32
    peers = [flip_bits(device, mask) for mask in range(COUNT)]
    high_bit = device // NEAR
    far = range(NEAR, COUNT)
    near = range(1, NEAR)

    barrier = pltpu.get_barrier_semaphore()
    for mask in range(1, COUNT):
        pl.semaphore_signal(
            barrier, inc=1, device_id={"ctx": peers[mask]}, device_id_type=pl.DeviceIdType.MESH
        )
    pl.semaphore_signal(
        barrier, inc=1, device_id={"groups": 1 - group}, device_id_type=pl.DeviceIdType.MESH
    )

    def lanes(index):
        return pl.ds(pl.multiple_of(index * block, block), block)

    def remote(kind, mask, src, dst, slot=None):
        slot = mask if slot is None else slot
        return pltpu.make_async_remote_copy(
            src_ref=src,
            dst_ref=dst,
            send_sem=send_sem.at[kind, slot],
            recv_sem=recv_sem.at[kind, slot],
            device_id={"ctx": peers[mask]},
            device_id_type=pl.DeviceIdType.MESH,
        )

    own = [
        pltpu.make_async_copy(values_hbm.at[:, lanes(device)], got_values.at[device], own_sem.at[0]),
        pltpu.make_async_copy(
            filter_hbm.at[:, :, :, lanes(device)], got_filter.at[:, :, device], own_sem.at[1]
        ),
        pltpu.make_async_copy(stream_hbm.at[:, lanes(device)], got_gate.at[device], own_sem.at[2]),
        pltpu.make_async_copy(tables_hbm, tables_ref, own_sem.at[3]),
        pltpu.make_async_copy(twist_hbm, twist_ref, own_sem.at[4]),
    ]
    weights = [
        pltpu.make_async_copy(src, dst, weight_sem.at[i])
        for i, (src, dst) in enumerate(((wg_hbm, wg), (wu_hbm, wu), (wd_hbm, wd)))
    ]
    for copy in own:
        copy.start()

    values_copy, filter_copy, gate_copy, passed = {}, {}, {}, {}
    for mask in range(1, COUNT):
        values_copy[mask] = remote(
            VALUES, mask, values_hbm.at[:, lanes(peers[mask])], got_values.at[device]
        )
        gate_copy[mask] = remote(
            GATE, mask, stream_hbm.at[:, lanes(peers[mask])], got_gate.at[device]
        )
        if mask < WHOLE:
            filter_copy[mask] = remote(
                FILTER, mask, filter_hbm.at[:, :, :, lanes(peers[mask])], got_filter.at[:, :, device]
            )
        else:
            filter_copy[mask] = remote(
                FILTER, mask, filter_hbm.at[:, group, :, lanes(peers[mask])], got_filter.at[:, group, device]
            )
            slab = got_filter.at[:, group, peers[mask]]
            passed[mask] = pltpu.make_async_remote_copy(
                src_ref=slab,
                dst_ref=slab,
                send_sem=send_sem.at[PASS, mask],
                recv_sem=recv_sem.at[PASS, mask],
                device_id={"groups": 1 - group},
                device_id_type=pl.DeviceIdType.MESH,
            )
    routes = [
        remote(ROUTE, NEAR, ids_ref, mirror_ids, 0),
        remote(ROUTE, NEAR, picks_ref, mirror_picks, 1),
    ]

    pl.semaphore_wait(barrier, COUNT)
    for mask in far:
        values_copy[mask].start()
        if mask > NEAR:
            values_copy[mask - NEAR].start()
    early = range(NEAR, NEAR + NEAR // 2)
    late = range(NEAR + NEAR // 2, COUNT)
    for mask in (*early, *near):
        filter_copy[mask].start()
    for copy in routes:
        copy.start()
    for copy in weights:
        copy.start()
    for mask in (*near, *far):
        values_copy[mask].wait_recv()
    for mask in late:
        filter_copy[mask].start()
    for mask in near:
        gate_copy[mask].start()
    for copy in own:
        copy.wait()

    def reverse(index):
        return int(reverse_bits(COUNT)[index])

    half = tokens
    tile = 16

    def spread(step):
        here = pl.ds(pl.multiple_of(step * tile, tile), tile)
        there = pl.ds(pl.multiple_of(half + step * tile, tile), tile)
        samples = [got_values[source, here, :].astype(f32) for source in range(COUNT)]
        zero = jnp.zeros_like(samples[0])
        for parity in range(2):
            pairs = [
                times_root((item, None), -source * parity, 2 * COUNT)
                for source, item in enumerate(samples)
            ]
            pairs = [(re, zero if im is None else im) for re, im in pairs]
            waves = short_transform(pairs, -1)
            for place in range(COUNT):
                re, im = waves[reverse(place)]
                column = 2 * place + parity
                cos = twist_ref[here, column : column + 1]
                sin = twist_ref[here, 2 * COUNT + column : 2 * COUNT + column + 1]
                for span, item in ((here, re * cos - im * sin), (there, re * sin + im * cos)):
                    high = item.astype(bf16)
                    columns = slice(column * block, (column + 1) * block)
                    wave_high[span, columns] = high
                    wave_low[span, columns] = (item - high.astype(f32)).astype(bf16)

    def hand_on(mask):
        filter_copy[mask].wait_recv()
        if mask >= WHOLE:
            passed[mask].start()

    pl.loop(0, tokens // tile // 2)(spread)
    for mask in near:
        hand_on(mask)
    pl.loop(tokens // tile // 2, tokens // tile)(spread)

    def product(which, columns):
        high, low = wave_high[:, columns], wave_low[:, columns]
        return (
            jnp.dot(tables_ref[which], high, preferred_element_type=f32)
            + jnp.dot(tables_ref[which], low, preferred_element_type=f32)
            + jnp.dot(tables_ref[which + 1], high, preferred_element_type=f32)
        )

    width = 4 * block

    @pl.loop(0, 2 * channels // width)
    def _(step):
        columns = pl.ds(pl.multiple_of(step * width, width), width)
        signal[0 : 2 * half, columns] = product(0, columns)

    def filter_places(first, number):
        @pl.loop(0, number // 2)
        def _(step):
            columns, highs, lows = [], [], []
            for mask in (first + 2 * step, first + 2 * step + 1):
                place = 0
                for bit in (1, 2, 4, 8):
                    place = place + bit * ((device // bit + mask // bit) % 2)
                columns.append(pl.ds(pl.multiple_of(2 * place * block, 2 * block), 2 * block))
                for parity in range(2):
                    lane = pl.ds(pl.multiple_of((2 * place + parity) * block, block), block)
                    re, im = signal[0:half, lane], signal[half : 2 * half, lane]
                    filter_re = got_filter[0, parity, place].astype(f32)
                    filter_im = got_filter[1, parity, place].astype(f32)
                    item = jnp.concatenate(
                        [re * filter_re - im * filter_im, re * filter_im + im * filter_re], axis=0
                    )
                    high = item.astype(bf16)
                    highs.append(high)
                    lows.append((item - high.astype(f32)).astype(bf16))
            high, low = jnp.concatenate(highs, axis=1), jnp.concatenate(lows, axis=1)
            value = (
                jnp.dot(tables_ref[2], high, preferred_element_type=f32)
                + jnp.dot(tables_ref[2], low, preferred_element_type=f32)
                + jnp.dot(tables_ref[3], high, preferred_element_type=f32)
            )
            for i, column in enumerate(columns):
                signal[0 : 2 * half, column] = value[:, 2 * i * block : 2 * (i + 1) * block]

    for mask in early:
        hand_on(mask)
    for mask in near:
        if mask >= WHOLE:
            passed[mask].wait_recv()
    filter_places(0, NEAR)
    for mask in late:
        hand_on(mask)
        gate_copy[mask].start()
        gate_copy[mask - NEAR // 2].start()
    for first in range(NEAR, COUNT, 2):
        for mask in (first, first + 1):
            passed[mask].wait_recv()
        filter_places(first, 2)
    scale = 1.0 / (2 * COUNT * tokens)

    def gather(step):
        here = pl.ds(pl.multiple_of(step * tile, tile), tile)
        there = pl.ds(pl.multiple_of(half + step * tile, tile), tile)
        sums = None
        for parity in range(2):
            waves = [None] * COUNT
            for place in range(COUNT):
                column = 2 * place + parity
                columns = slice(column * block, (column + 1) * block)
                re, im = signal[here, columns], signal[there, columns]
                cos = twist_ref[here, column : column + 1]
                sin = twist_ref[here, 2 * COUNT + column : 2 * COUNT + column + 1]
                waves[reverse(place)] = (re * cos + im * sin, im * cos - re * sin)
            pairs = short_transform(waves, 1)
            parts = [times_root(pair, source * parity, 2 * COUNT)[0] for source, pair in enumerate(pairs)]
            sums = parts if sums is None else [left + right for left, right in zip(sums, parts)]
        for source in range(COUNT):
            result[source, here, :] = sums[source] * scale

    pl.loop(0, tokens // tile)(gather)

    mirror_copy, owner_copy = {}, {}
    for mask in range(1, COUNT):
        mirror_copy[mask] = remote(
            MIRROR, mask, blocks.at[(mask + NEAR) % COUNT], mirror_rows.at[:, lanes(device)]
        )
        owner_copy[mask] = remote(OWNER, mask, blocks.at[mask], own_rows.at[:, lanes(device)])

    def make_block(mask):
        source = peers[mask]
        blocks[mask] = (result[source] * got_gate[source].astype(f32)).astype(bf16)

    for mask in range(NEAR):
        if mask:
            gate_copy[mask].wait_recv()
        make_block(mask)
        mirror_copy[mask + NEAR].start()
        if mask:
            owner_copy[mask].start()
    own_rows[:, lanes(device)] = blocks[0]
    for mask in range(NEAR):
        gate_copy[mask + NEAR].wait_recv()
        make_block(mask + NEAR)
        if mask:
            mirror_copy[mask].start()
    mirror_rows[:, lanes(device)] = blocks[NEAR]
    for copy in routes:
        copy.wait()

    near_rows = NEAR * HEAD
    columns_of = [
        pl.ds(pl.multiple_of(base * half_channels, half_channels), half_channels)
        for base in (high_bit, 1 - high_bit)
    ]

    def part_of(chunk, part):
        base = (high_bit, 1 - high_bit)[chunk] * half_channels + part * part_width
        return pl.ds(pl.multiple_of(base, part_width), part_width)

    def targets_of(ids, picks):
        position = jnp.full_like(ids, -1024)
        for mask in range(COUNT):
            position = jnp.where(ids == peers[mask], mask * HEAD, position)
        head = jnp.where(picks < HEAD, position + picks, -1024)
        tail = jnp.where((picks >= HEAD) & (picks < CAP), position + picks - HEAD, -1024)
        return head, tail

    slot_row = lax.broadcasted_iota(jnp.int32, (near_rows, tokens), 0)

    def hits(targets, shift):
        return [slot_row == targets[pick : pick + 1, :] + shift for pick in range(2)]

    def one_hot(targets, shift):
        first, second = hits(targets, shift)
        return jnp.where(first | second, 1.0, 0.0).astype(bf16)

    send_copy = {}
    for kind in range(2):
        for chunk in range(2):
            buffer = 2 * kind + chunk
            for mask in range(NEAR):
                span = pl.ds(mask * HEAD, HEAD)
                src, dst = packed.at[buffer, span], arrived.at[buffer, span]
                if mask:
                    send_copy[buffer, mask] = remote(SEND + buffer, mask, src, dst)
                else:
                    send_copy[buffer, mask] = pltpu.make_async_copy(src, dst, own_sem.at[buffer])

    def dispatch(kind, chunk, source, targets):
        head, tail = targets
        buffer = 2 * kind + chunk
        packed[buffer, :, 0:half_channels] = jnp.dot(
            one_hot(head, 0), source[:, columns_of[chunk]], preferred_element_type=f32
        ).astype(bf16)
        tails = jnp.zeros((near_rows, part_width), f32)
        for part in range(PARTS):
            tails = tails + jnp.dot(
                one_hot(tail, TAIL * part), source[:, part_of(chunk, part)], preferred_element_type=f32
            )
        packed[buffer, :, half_channels:] = tails.astype(bf16)
        for mask in reversed(range(NEAR)):
            send_copy[buffer, mask].start()

    mirror_targets = targets_of(mirror_ids[...], mirror_picks[...])
    for mask in near:
        mirror_copy[mask].wait_recv()
    dispatch(0, 0, mirror_rows, mirror_targets)
    own_targets = targets_of(ids_ref[...], picks_ref[...])

    def dispatch_near():
        for mask in near:
            owner_copy[mask].wait_recv()
        dispatch(1, 0, own_rows, own_targets)

    def dispatch_far():
        for mask in far:
            owner_copy[mask].wait_recv()
        dispatch(1, 1, own_rows, own_targets)

    for mask in far:
        mirror_copy[mask].wait_recv()
    dispatch(0, 1, mirror_rows, mirror_targets)
    dispatch_near()
    for mask in far:
        owner_copy[mask].start()

    tail_rows = NEAR * TAIL
    pick_row = lax.broadcasted_iota(jnp.int32, (tail_rows, near_rows), 0)
    pick_col = lax.broadcasted_iota(jnp.int32, (tail_rows, near_rows), 1)
    pick_base = (pick_row // TAIL) * HEAD + pick_row % TAIL

    def selection(part):
        return jnp.where(pick_col == pick_base + TAIL * part, 1.0, 0.0).astype(bf16)

    back_row = lax.broadcasted_iota(jnp.int32, (near_rows, tail_rows), 0)
    back_col = lax.broadcasted_iota(jnp.int32, (near_rows, tail_rows), 1)
    back_base = (back_col // TAIL) * HEAD + back_col % TAIL

    def placing(part):
        return jnp.where(back_row == back_base + TAIL * part, 1.0, 0.0).astype(bf16)

    back_copy = {}
    for chunk in range(BACKS):
        for mask in range(COUNT):
            kind = 0 if mask >= NEAR else 1
            src = done.at[BACKS * kind + chunk, pl.ds(mask % NEAR * HEAD, HEAD)]
            dst = back.at[chunk, pl.ds(mask * HEAD, HEAD)]
            if mask:
                back_copy[chunk, mask] = remote(BACK + chunk, mask, src, dst)
            else:
                back_copy[chunk, mask] = pltpu.make_async_copy(src, dst, own_sem.at[4 + chunk])

    def normalise(source, destination, count):
        @pl.loop(0, count // tile)
        def _(step):
            here = pl.ds(pl.multiple_of(step * tile, tile), tile)
            item = source[here, :].astype(f32)
            mean = jnp.sum(item * item, axis=1, keepdims=True) / channels
            destination[here, :] = (item * lax.rsqrt(mean + 1e-06)).astype(bf16)

    group_rows = near_rows + tail_rows
    wide = 256
    back_width = channels // BACKS
    back_part = back_width // PARTS

    def take(kind, chunk):
        buffer = 2 * kind + chunk
        for mask in range(NEAR):
            if mask:
                send_copy[buffer, mask].wait_recv()
            else:
                send_copy[buffer, mask].wait()
        rows[0:near_rows, columns_of[chunk]] = arrived[buffer, :, 0:half_channels]
        for part in range(PARTS):
            rows[near_rows:group_rows, part_of(chunk, part)] = jnp.dot(
                selection(part), arrived[buffer, :, half_channels:], preferred_element_type=f32
            ).astype(bf16)

    def squares(chunk):
        @pl.loop(0, group_rows // tile)
        def _(step):
            here = pl.ds(pl.multiple_of(step * tile, tile), tile)
            item = rows[here, columns_of[chunk]].astype(f32)
            part = jnp.sum(item * item, axis=1, keepdims=True)
            if chunk == 0:
                inverse[here, :] = jnp.broadcast_to(part, (tile, wide))
            else:
                mean = (inverse[here, :] + part) / channels
                inverse[here, :] = lax.rsqrt(mean + 1e-06)

    def expert(kind):
        take(kind, 0)
        if kind == 0:
            weights[0].wait()
            weights[1].wait()

        @pl.loop(0, hidden_size // wide)
        def _(step):
            columns = pl.ds(pl.multiple_of(step * wide, wide), wide)
            item = rows[:, columns_of[0]]
            signal[0:group_rows, columns] = jnp.dot(
                item, wg[columns_of[0], columns], preferred_element_type=f32
            )
            signal[group_rows : 2 * group_rows, columns] = jnp.dot(
                item, wu[columns_of[0], columns], preferred_element_type=f32
            )

        squares(0)
        take(kind, 1)
        squares(1)

        def pair(step):
            columns = pl.ds(pl.multiple_of(step * wide, wide), wide)
            item = rows[:, columns_of[1]]
            gate_part = signal[0:group_rows, columns] + jnp.dot(
                item, wg[columns_of[1], columns], preferred_element_type=f32
            )
            up_part = signal[group_rows : 2 * group_rows, columns] + jnp.dot(
                item, wu[columns_of[1], columns], preferred_element_type=f32
            )
            return gate_part, up_part

        def keep(slot, parts):
            gate_sum[slot], up_sum[slot] = parts

        def activate(step, slot):
            columns = pl.ds(pl.multiple_of(step * wide, wide), wide)
            scales = inverse[...]
            hidden[:, columns] = (
                jax.nn.silu(gate_sum[slot] * scales) * (up_sum[slot] * scales)
            ).astype(bf16)

        last = hidden_size // wide - 1
        keep(0, pair(0))

        @pl.loop(0, last // 2)
        def _(step):
            for odd in range(2):
                parts = pair(2 * step + odd + 1)
                activate(2 * step + odd, odd)
                keep(1 - odd, parts)

        if last % 2:
            parts = pair(last)
            activate(last - 1, 0)
            keep(1, parts)
        activate(last, last % 2)

        if kind == 0:
            weights[2].wait()
        steps = half_channels * 2 // BACKS // wide
        for chunk in range(BACKS):
            buffer = BACKS * kind + chunk
            tail_sum[...] = jnp.zeros_like(tail_sum)

            @pl.loop(0, steps)
            def _(step):
                inner = pl.ds(pl.multiple_of(step * wide, wide), wide)
                columns = pl.ds(pl.multiple_of((chunk * steps + step) * wide, wide), wide)
                value = jnp.dot(hidden[...], wd[:, columns], preferred_element_type=f32).astype(bf16)
                done[buffer, :, inner] = value[0:near_rows, :]
                tails = tail_sum[...]
                for side in range(wide // back_part):
                    tails = tails + jnp.dot(
                        placing(step * (wide // back_part) + side),
                        value[near_rows:group_rows, side * back_part : (side + 1) * back_part],
                        preferred_element_type=f32,
                    )
                tail_sum[...] = tails

            done[buffer, :, back_width:] = tail_sum[...].astype(bf16)
            for mask in far if kind == 0 else range(NEAR):
                back_copy[chunk, mask].start()
            if kind == 0 and chunk == BACKS // 2 - 1:
                dispatch_far()

    expert(0)
    normalise(own_rows, normed, tokens)
    logits = lax.dot_general(
        router_ref[...], normed[...], (((1,), (1,)), ((), ())), preferred_element_type=f32
    )
    expert_row = lax.broadcasted_iota(jnp.int32, logits.shape, 0)
    for pick in range(2):
        chosen = jnp.sum(
            jnp.where(expert_row == ids_ref[pick : pick + 1, :], logits, 0.0), axis=0, keepdims=True
        )
        gates[pick : pick + 1, :] = jax.nn.sigmoid(chosen)
    expert(1)

    def weights_of(targets, shift):
        first, second = hits(targets, shift)
        mix = jnp.where(first, gates[0:1, :], 0.0) + jnp.where(second, gates[1:2, :], 0.0)
        mix = mix.T
        high = mix.astype(bf16)
        return high, (mix - high.astype(f32)).astype(bf16)

    def weighted(pair, values):
        return sum(jnp.dot(piece, values, preferred_element_type=f32) for piece in pair)

    head, tail = own_targets
    for side in range(2):
        shift = -side * near_rows
        span = slice(side * near_rows, (side + 1) * near_rows)
        head_pair = weights_of(head, shift)
        tail_pairs = [weights_of(tail, shift + TAIL * part) for part in range(PARTS)]
        for chunk in range(BACKS):
            for mask in range(side * NEAR, (side + 1) * NEAR):
                if mask:
                    back_copy[chunk, mask].wait_recv()
                else:
                    back_copy[chunk, mask].wait()
            columns = slice(chunk * back_width, (chunk + 1) * back_width)
            added = weighted(head_pair, back[chunk, span, 0:back_width]) + jnp.concatenate(
                [weighted(pair, back[chunk, span, back_width:]) for pair in tail_pairs], axis=1
            )
            if side == 0:
                total[:, columns] = own_rows[:, columns].astype(f32) + added
            else:
                out_ref[:, columns] = (total[:, columns] + added).astype(bf16)

    for mask in range(1, COUNT):
        values_copy[mask].wait_send()
        filter_copy[mask].wait_send()
        gate_copy[mask].wait_send()
        mirror_copy[mask].wait_send()
        owner_copy[mask].wait_send()
        if mask >= WHOLE:
            passed[mask].wait_send()
        for chunk in range(BACKS):
            back_copy[chunk, mask].wait_send()
    for buffer in range(4):
        for mask in near:
            send_copy[buffer, mask].wait_send()


def run_layer(
    value_stream, gate_stream, filter_spectrum, router, w_gate, w_up, w_down, route_ids, route_slots
):
    tokens, channels = value_stream.shape
    hidden_size = w_gate.shape[1]
    block = channels // COUNT
    near_rows = NEAR * HEAD
    half_rows = near_rows + NEAR * TAIL
    part_width = channels // 2 // PARTS
    packed_width = channels // 2 + part_width
    back_width = channels // BACKS + channels // BACKS // PARTS
    vmem = pl.BlockSpec(memory_space=pltpu.VMEM)
    hbm = pl.BlockSpec(memory_space=pl.ANY)
    bf16, f32, i32 = jnp.bfloat16, jnp.float32, jnp.int32
    return pl.pallas_call(
        layer_kernel,
        out_shape=jax.ShapeDtypeStruct((tokens, channels), bf16),
        in_specs=[hbm] * 5 + [vmem] * 3 + [hbm] * 3,
        out_specs=vmem,
        scratch_shapes=[
            pltpu.VMEM((4, 2 * tokens, 2 * tokens), bf16),
            pltpu.VMEM((tokens, 4 * COUNT), f32),
            pltpu.VMEM((COUNT, tokens, block), bf16),
            pltpu.VMEM((2, 2, COUNT, tokens, block), bf16),
            pltpu.VMEM((COUNT, tokens, block), bf16),
            pltpu.VMEM((2 * tokens, 2 * channels), bf16),
            pltpu.VMEM((2 * tokens, 2 * channels), bf16),
            pltpu.VMEM((max(2 * tokens, 2 * half_rows), 2 * channels), f32),
            pltpu.VMEM((COUNT, tokens, block), f32),
            pltpu.VMEM((COUNT, tokens, block), bf16),
            pltpu.VMEM((tokens, channels), bf16),
            pltpu.VMEM((tokens, channels), bf16),
            pltpu.VMEM((tokens, channels), bf16),
            pltpu.VMEM((2, tokens), i32),
            pltpu.VMEM((2, tokens), i32),
            pltpu.VMEM((4, near_rows, packed_width), bf16),
            pltpu.VMEM((4, near_rows, packed_width), bf16),
            pltpu.VMEM((half_rows, channels), bf16),
            pltpu.VMEM((half_rows, hidden_size), bf16),
            pltpu.VMEM((channels, hidden_size), bf16),
            pltpu.VMEM((channels, hidden_size), bf16),
            pltpu.VMEM((hidden_size, channels), bf16),
            pltpu.VMEM((half_rows, 256), f32),
            pltpu.VMEM((2, half_rows, 256), f32),
            pltpu.VMEM((2, half_rows, 256), f32),
            pltpu.VMEM((2 * BACKS, near_rows, back_width), bf16),
            pltpu.VMEM((BACKS, 2 * near_rows, back_width), bf16),
            pltpu.VMEM((near_rows, channels // BACKS // PARTS), f32),
            pltpu.VMEM((8, tokens), f32),
            pltpu.VMEM((tokens, channels), f32),
            pltpu.SemaphoreType.DMA((4 + BACKS,)),
            pltpu.SemaphoreType.DMA((KINDS, COUNT)),
            pltpu.SemaphoreType.DMA((KINDS, COUNT)),
            pltpu.SemaphoreType.DMA((3,)),
        ],
        compiler_params=pltpu.CompilerParams(
            collective_id=1, has_side_effects=True, vmem_limit_bytes=63 * 1024 * 1024
        ),
    )(
        value_stream, gate_stream, filter_spectrum, inner_tables(tokens), twist_table(COUNT, tokens),
        router.T, route_ids, route_slots, w_gate, w_up, w_down,
    )


def local(
    value_stream, gate_stream, filter_spectrum, router, w_gate, w_up, w_down, route_ids, route_slots
):
    tok_rows, channels = value_stream.shape
    size_ctx = lax.axis_size("ctx")
    block = channels // size_ctx
    expert_count = router.shape[1]
    if (
        size_ctx == expert_count == COUNT
        and lax.axis_size("groups") == 2
        and block == tok_rows == 128
        and w_gate.shape[1] % 256 == 0
    ):
        return run_layer(
            value_stream, gate_stream, filter_spectrum, router, w_gate, w_up, w_down, route_ids, route_slots
        )
    arrived = lax.all_to_all(value_stream, "ctx", split_axis=1, concat_axis=0, tiled=True)
    filter_all = lax.all_to_all(filter_spectrum, "ctx", split_axis=3, concat_axis=2, tiled=True)
    long_conv = convolve(arrived, filter_all, size_ctx, tok_rows, block)
    long_conv = lax.all_to_all(
        long_conv.astype(jnp.bfloat16), "ctx", split_axis=0, concat_axis=1, tiled=True
    )
    long_conv = long_conv.astype(jnp.float32)
    hyena_out = (gate_stream.astype(jnp.float32) * long_conv).astype(jnp.bfloat16)
    hyena32 = hyena_out.astype(jnp.float32)
    inv_rms = lax.rsqrt(jnp.mean(hyena32 * hyena32, axis=1, keepdims=True) + 1e-06)
    normed = (hyena32 * inv_rms).astype(jnp.bfloat16)
    logits = jnp.dot(normed, router, preferred_element_type=jnp.float32)
    owner_split = size_ctx // expert_count
    slot_count = expert_count * CAP
    positions = jnp.arange(slot_count, dtype=jnp.int32)
    expert_range = jnp.arange(expert_count, dtype=jnp.int32)
    combine = jnp.zeros((tok_rows, slot_count), jnp.float32)
    dispatch = jnp.zeros((slot_count, channels), jnp.float32)
    for pick_index in range(route_ids.shape[0]):
        expert_ids = route_ids[pick_index]
        slot_ids = route_slots[pick_index]
        target = jnp.where(slot_ids < CAP, expert_ids * CAP + slot_ids, -1)
        slot_hits = target[:, None] == positions[None, :]
        chosen_logit = jnp.sum(
            jnp.where(expert_ids[:, None] == expert_range[None, :], logits, 0.0), axis=1
        )
        gate_value = jax.nn.sigmoid(chosen_logit)
        combine = combine + slot_hits.astype(jnp.float32) * gate_value[:, None]
        dispatch = dispatch + lax.dot_general(
            slot_hits.astype(jnp.bfloat16),
            normed,
            (((0,), (0,)), ((), ())),
            preferred_element_type=jnp.float32,
        )
    buffer = dispatch.astype(jnp.bfloat16).reshape(expert_count, CAP, channels)
    outgoing = jnp.repeat(buffer, owner_split, axis=0)
    slot_rows = lax.all_to_all(outgoing, "ctx", split_axis=0, concat_axis=0, tiled=True)
    flat_rows = slot_rows.reshape(-1, channels)
    gate_part = jnp.dot(flat_rows, w_gate, preferred_element_type=jnp.float32)
    up_part = jnp.dot(flat_rows, w_up, preferred_element_type=jnp.float32)
    hidden = (jax.nn.silu(gate_part) * up_part).astype(jnp.bfloat16)
    partial_value = jnp.dot(hidden, w_down, preferred_element_type=jnp.float32).astype(jnp.bfloat16)
    returned = lax.all_to_all(
        partial_value.reshape(slot_rows.shape), "ctx", split_axis=0, concat_axis=0, tiled=True
    )
    expert_out = jnp.sum(
        returned.astype(jnp.float32).reshape(expert_count, owner_split, CAP, channels), axis=1
    ).reshape(slot_count, channels)
    contribution = jnp.dot(combine, expert_out, precision=highest)
    return (hyena32 + contribution).astype(jnp.bfloat16)


def solution(mesh):
    in_specs = (
        P(("groups", "ctx"), None),
        P(("groups", "ctx"), None),
        P(None, None, "ctx", None),
        P(),
        P(None, "ctx"),
        P(None, "ctx"),
        P("ctx", None),
        P(None, ("groups", "ctx")),
        P(None, ("groups", "ctx")),
    )
    out_specs = P(("groups", "ctx"), None)
    return jax.shard_map(local, mesh=mesh, in_specs=in_specs, out_specs=out_specs, check_vma=False)
```

```python
import jax
import jax.numpy as jnp
import numpy as np
from jax import lax
from jax.experimental import pallas as pl
from jax.experimental.pallas import tpu as pltpu
from jax.sharding import PartitionSpec as P

CAP = 20


two_pi = 2.0 * np.pi
highest = lax.Precision.HIGHEST


def reverse_bits(length_n):
    bit_count = length_n.bit_length() - 1
    positions = np.arange(length_n)
    reversed_index = np.zeros(length_n, dtype=np.int64)
    for position in range(bit_count):
        reversed_index = reversed_index | (positions >> position & 1) << bit_count - 1 - position
    return reversed_index


def spread_table(size_ctx):
    rho = 2 * reverse_bits(size_ctx)[None, :] + np.arange(2)[:, None]
    angle_rad = -two_pi * (np.outer(rho.reshape(-1), np.arange(size_ctx)) % (2 * size_ctx)) / (2 * size_ctx)
    parts = np.stack([np.cos(angle_rad), np.sin(angle_rad)], axis=1)
    return jnp.asarray(parts, jnp.float32)


def fine_table(size_ctx, tok_rows):
    total = 2 * size_ctx * tok_rows
    rho = (2 * reverse_bits(size_ctx)[None, :] + np.arange(2)[:, None]).reshape(-1)
    k = 2 * size_ctx * reverse_bits(tok_rows)[None, :] + rho[:, None]
    step = (k[:, :, None] * np.arange(tok_rows)[None, None, :]) % total
    angle_rad = -two_pi * step / total
    re, im = np.cos(angle_rad), np.sin(angle_rad)
    table = np.stack([np.stack([re, -im], axis=2), np.stack([im, re], axis=2)], axis=1)
    return jnp.asarray(table.reshape(2 * size_ctx, 2 * tok_rows, 2 * tok_rows), jnp.float32)


def convolve(arrived, filter_all, size_ctx, tok_rows, block):
    rho_count = 2 * size_ctx
    coarse = spread_table(size_ctx)
    fine = fine_table(size_ctx, tok_rows)
    samples = arrived.astype(jnp.float32).reshape(size_ctx, tok_rows * block)
    spread = jnp.dot(coarse.reshape(2 * rho_count, size_ctx), samples, precision=highest)
    spread = spread.reshape(rho_count, 2 * tok_rows, block)
    signal = jnp.einsum("rqt,rtc->rqc", fine, spread, precision=highest)
    signal = signal.reshape(rho_count, 2, tok_rows, block)
    filter32 = filter_all.astype(jnp.float32).reshape(2, rho_count, tok_rows, block)
    real_part = signal[:, 0] * filter32[0] - signal[:, 1] * filter32[1]
    imag_part = signal[:, 0] * filter32[1] + signal[:, 1] * filter32[0]
    signal = jnp.concatenate([real_part, imag_part], axis=1)
    spread = jnp.einsum("rqt,rqc->rtc", fine, signal, precision=highest)
    spread = spread.reshape(2 * rho_count, tok_rows * block)
    folded = jnp.dot(coarse.reshape(2 * rho_count, size_ctx).T, spread, precision=highest)
    return (folded / (rho_count * tok_rows)).reshape(size_ctx * tok_rows, block)


def flip_bits(index, mask):
    result = index
    bit = 1
    while bit <= mask:
        if mask & bit:
            result = result + bit * (1 - 2 * ((index // bit) % 2))
        bit *= 2
    return result


COUNT = 16
NEAR = COUNT // 2
HEAD = 16
TAIL = CAP - HEAD
PARTS = HEAD // TAIL


def twist_table(size_ctx, tok_rows):
    rho = (2 * reverse_bits(size_ctx)[:, None] + np.arange(2)[None, :]).reshape(-1)
    angle_rad = -two_pi * np.outer(np.arange(tok_rows), rho) / (2 * size_ctx * tok_rows)
    return jnp.asarray(np.concatenate([np.cos(angle_rad), np.sin(angle_rad)], axis=1), jnp.float32)


def inner_tables(tok_rows):
    angle_rad = -two_pi * (np.outer(reverse_bits(tok_rows), np.arange(tok_rows)) % tok_rows) / tok_rows
    re, im = np.cos(angle_rad), np.sin(angle_rad)
    table = np.block([[re, -im], [im, re]]).astype(np.float32)
    pieces = []
    for matrix in (table, table.T):
        high = matrix.astype(jnp.bfloat16)
        low = (matrix - high.astype(np.float32)).astype(jnp.bfloat16)
        pieces += [high, low]
    return jnp.asarray(np.stack(pieces))


def times_root(pair, power, order):
    power %= order
    re, im = pair
    if power == 0:
        return pair
    if im is None and 4 * power % order:
        cos, sin = float(np.cos(two_pi * power / order)), float(np.sin(two_pi * power / order))
        return (re * cos, re * sin)
    if im is None:
        im = jnp.zeros_like(re)
    if 4 * power == order:
        return (-im, re)
    if 2 * power == order:
        return (-re, -im)
    if 4 * power == 3 * order:
        return (im, -re)
    cos, sin = float(np.cos(two_pi * power / order)), float(np.sin(two_pi * power / order))
    return (re * cos - im * sin, re * sin + im * cos)


def short_transform(values, sign):
    order = len(values)
    if order == 1:
        return values
    even = short_transform(values[0::2], sign)
    odd = short_transform(values[1::2], sign)
    turned = [times_root(odd[i], sign * i, order) for i in range(order // 2)]
    return [(even[i][0] + turned[i][0], even[i][1] + turned[i][1]) for i in range(order // 2)] + [
        (even[i][0] - turned[i][0], even[i][1] - turned[i][1]) for i in range(order // 2)
    ]


VALUES, FILTER, GATE, MIRROR, OWNER, SEND, BACK, ROUTE, PASS, PAIR, FOLD = 0, 1, 2, 3, 4, 5, 9, 13, 14, 15, 16
KINDS = 17
BACKS = 4
WHOLE = 4


def layer_kernel(
    values_hbm, stream_hbm, filter_hbm, tables_hbm, twist_hbm, router_ref, ids_ref, picks_ref, wg_hbm, wu_hbm, wd_hbm,
    out_ref,
    tables_ref, twist_ref, got_values, got_filter, got_gate, pair_rows, own_pair, folded, wave_high, wave_low, signal, result, blocks,
    own_rows, mirror_rows, normed, mirror_ids, mirror_picks, packed, arrived, rows, hidden, wg, wu, wd,
    inverse, gate_sum, up_sum, done, back, tail_sum, gates, total, own_sem, send_sem, recv_sem, weight_sem, pair_sem,
):
    device = lax.axis_index("ctx")
    group = lax.axis_index("groups")
    tokens, channels = own_rows.shape
    block = channels // COUNT
    half_channels = channels // 2
    part_width = half_channels // PARTS
    hidden_size = wg.shape[1]
    bf16, f32 = jnp.bfloat16, jnp.float32
    peers = [flip_bits(device, mask) for mask in range(COUNT)]
    high_bit = device // NEAR
    far = range(NEAR, COUNT)
    near = range(1, NEAR)

    barrier = pltpu.get_barrier_semaphore()
    for mask in range(1, COUNT):
        pl.semaphore_signal(
            barrier, inc=1, device_id={"ctx": peers[mask]}, device_id_type=pl.DeviceIdType.MESH
        )
    pl.semaphore_signal(
        barrier, inc=1, device_id={"groups": 1 - group}, device_id_type=pl.DeviceIdType.MESH
    )

    def lanes(index):
        return pl.ds(pl.multiple_of(index * block, block), block)

    def remote(kind, mask, src, dst, slot=None):
        slot = mask if slot is None else slot
        return pltpu.make_async_remote_copy(
            src_ref=src,
            dst_ref=dst,
            send_sem=send_sem.at[kind, slot],
            recv_sem=recv_sem.at[kind, slot],
            device_id={"ctx": peers[mask]},
            device_id_type=pl.DeviceIdType.MESH,
        )

    own = [
        pltpu.make_async_copy(values_hbm.at[:, lanes(device)], got_values.at[device], own_sem.at[0]),
        pltpu.make_async_copy(
            filter_hbm.at[:, :, :, lanes(device)], got_filter.at[:, :, device], own_sem.at[1]
        ),
        pltpu.make_async_copy(stream_hbm.at[:, lanes(device)], got_gate.at[device], own_sem.at[2]),
        pltpu.make_async_copy(tables_hbm, tables_ref, own_sem.at[3]),
        pltpu.make_async_copy(twist_hbm, twist_ref, own_sem.at[4]),
    ]
    weights = [
        pltpu.make_async_copy(src, dst, weight_sem.at[i])
        for i, (src, dst) in enumerate(((wg_hbm, wg), (wu_hbm, wu), (wd_hbm, wd)))
    ]
    for copy in own:
        copy.start()

    values_copy, filter_copy, gate_copy, passed = {}, {}, {}, {}
    for mask in range(1, COUNT):
        values_copy[mask] = remote(
            VALUES, mask, values_hbm.at[:, lanes(peers[mask])], got_values.at[device]
        )
        gate_copy[mask] = remote(
            GATE, mask, stream_hbm.at[:, lanes(peers[mask])], got_gate.at[device]
        )
        if mask < WHOLE:
            filter_copy[mask] = remote(
                FILTER, mask, filter_hbm.at[:, :, :, lanes(peers[mask])], got_filter.at[:, :, device]
            )
        else:
            filter_copy[mask] = remote(
                FILTER, mask, filter_hbm.at[:, group, :, lanes(peers[mask])], got_filter.at[:, group, device]
            ) if mask < NEAR else remote(
                FILTER, mask, filter_hbm.at[group, 1, :, lanes(peers[mask])], got_filter.at[group, 1, device]
            )
            slab = got_filter.at[:, group, peers[mask]] if mask < NEAR else got_filter.at[group, :, peers[mask]]
            passed[mask] = pltpu.make_async_remote_copy(
                src_ref=slab,
                dst_ref=slab,
                send_sem=send_sem.at[PASS, mask],
                recv_sem=recv_sem.at[PASS, mask],
                device_id={"groups": 1 - group},
                device_id_type=pl.DeviceIdType.MESH,
            )
    core, level, line = device % 2, device // 4 % 2, device // 2 % 2
    partner_mask = high_bit * 7 + (1 - high_bit) * (level * 3 + (1 - level) * line)
    partner = 0
    for bit in (1, 2, 4):
        partner = partner + bit * ((device // bit + partner_mask // bit) % 2)
    partner = partner + NEAR * high_bit
    paired = device >= 2
    quarters = NEAR // 2
    pair_copy, own_pair_copy, fold_copy = [], [], {}
    for quarter in range(quarters):
        base = (1 - high_bit) * NEAR + 2 * quarter
        pair_copy.append(pltpu.make_async_remote_copy(
            src_ref=filter_hbm.at[group, 0, :, lanes(base + 1 - core)],
            dst_ref=pair_rows.at[quarter],
            send_sem=send_sem.at[PAIR, quarter],
            recv_sem=recv_sem.at[PAIR, quarter],
            device_id={"ctx": partner},
            device_id_type=pl.DeviceIdType.MESH,
        ))
        own_pair_copy.append(pltpu.make_async_copy(
            filter_hbm.at[group, 0, :, lanes(base + core)], own_pair.at[quarter], pair_sem.at[quarter]
        ))
    for mask in far:
        source = (
            filter_hbm.at[group, 0, :, lanes(peers[mask])] if mask % 2 else folded.at[peers[mask] // 2 % quarters]
        )
        fold_copy[mask] = remote(FOLD, mask, source, got_filter.at[group, 0, device])
    routes = [
        remote(ROUTE, NEAR, ids_ref, mirror_ids, 0),
        remote(ROUTE, NEAR, picks_ref, mirror_picks, 1),
    ]

    pl.semaphore_wait(barrier, COUNT)
    for mask in far:
        values_copy[mask].start()
        if mask > NEAR:
            values_copy[mask - NEAR].start()
    early = range(NEAR, NEAR + NEAR // 2)
    late = range(NEAR + NEAR // 2, COUNT)
    for copy in own_pair_copy:
        copy.start()

    @pl.when(paired)
    def _():
        for copy in pair_copy:
            copy.start()

    @pl.when(device < 2)
    def _():
        for mask in far:
            if mask % 2:
                fold_copy[mask].start()
        pair_rows[...] = jnp.zeros_like(pair_rows)

    for mask in (*early, *near):
        filter_copy[mask].start()
    for copy in routes:
        copy.start()
    for copy in weights:
        copy.start()
    for copy in own_pair_copy:
        copy.wait()

    @pl.when(paired)
    def _():
        for copy in pair_copy:
            copy.wait_recv()

    sign = (1 - 2 * group).astype(f32)
    flip_row = lax.broadcasted_iota(jnp.int32, (tokens, tokens), 0)
    flip_col = lax.broadcasted_iota(jnp.int32, (tokens, tokens), 1)
    flip = jnp.where(flip_row + flip_col == tokens - 1, 1.0, 0.0).astype(bf16)
    for quarter in range(quarters):
        turned = jnp.dot(flip, pair_rows[quarter], preferred_element_type=f32)
        folded[quarter] = (own_pair[quarter].astype(f32) + sign * turned).astype(bf16)
    for mask in far:
        if mask % 2 == 0:
            fold_copy[mask].start()
    for mask in (*near, *far):
        values_copy[mask].wait_recv()
    for mask in late:
        filter_copy[mask].start()
    for mask in near:
        gate_copy[mask].start()
    for copy in own:
        copy.wait()

    def reverse(index):
        return int(reverse_bits(COUNT)[index])

    half = tokens
    tile = 16

    def spread(step):
        here = pl.ds(pl.multiple_of(step * tile, tile), tile)
        there = pl.ds(pl.multiple_of(half + step * tile, tile), tile)
        samples = [got_values[source, here, :].astype(f32) for source in range(COUNT)]
        zero = jnp.zeros_like(samples[0])
        for parity in range(2):
            pairs = [
                times_root((item, None), -source * parity, 2 * COUNT)
                for source, item in enumerate(samples)
            ]
            pairs = [(re, zero if im is None else im) for re, im in pairs]
            waves = short_transform(pairs, -1)
            for place in range(COUNT):
                re, im = waves[reverse(place)]
                column = 2 * place + parity
                cos = twist_ref[here, column : column + 1]
                sin = twist_ref[here, 2 * COUNT + column : 2 * COUNT + column + 1]
                for span, item in ((here, re * cos - im * sin), (there, re * sin + im * cos)):
                    high = item.astype(bf16)
                    columns = slice(column * block, (column + 1) * block)
                    wave_high[span, columns] = high
                    wave_low[span, columns] = (item - high.astype(f32)).astype(bf16)

    def hand_on(mask):
        filter_copy[mask].wait_recv()
        if mask >= NEAR and mask % 2 == 0:
            fold_copy[mask].wait_recv()
        if mask >= NEAR and mask % 2:
            @pl.when(peers[mask] < 2)
            def _():
                fold_copy[mask].wait_recv()

            @pl.when(peers[mask] >= 2)
            def _():
                got_filter[group, 0, peers[mask]] = jnp.zeros((tokens, block), bf16)

        if mask >= WHOLE:
            passed[mask].start()

    pl.loop(0, tokens // tile // 2)(spread)
    for mask in near:
        hand_on(mask)
    pl.loop(tokens // tile // 2, tokens // tile)(spread)

    def product(which, columns):
        high, low = wave_high[:, columns], wave_low[:, columns]
        return (
            jnp.dot(tables_ref[which], high, preferred_element_type=f32)
            + jnp.dot(tables_ref[which], low, preferred_element_type=f32)
            + jnp.dot(tables_ref[which + 1], high, preferred_element_type=f32)
        )

    width = 4 * block

    @pl.loop(0, 2 * channels // width)
    def _(step):
        columns = pl.ds(pl.multiple_of(step * width, width), width)
        signal[0 : 2 * half, columns] = product(0, columns)

    def filter_places(first, number):
        @pl.loop(0, number // 2)
        def _(step):
            columns, highs, lows = [], [], []
            for mask in (first + 2 * step, first + 2 * step + 1):
                place = 0
                for bit in (1, 2, 4, 8):
                    place = place + bit * ((device // bit + mask // bit) % 2)
                columns.append(pl.ds(pl.multiple_of(2 * place * block, 2 * block), 2 * block))
                for parity in range(2):
                    lane = pl.ds(pl.multiple_of((2 * place + parity) * block, block), block)
                    re, im = signal[0:half, lane], signal[half : 2 * half, lane]
                    filter_re = got_filter[0, parity, place].astype(f32)
                    filter_im = got_filter[1, parity, place].astype(f32)
                    item = jnp.concatenate(
                        [re * filter_re - im * filter_im, re * filter_im + im * filter_re], axis=0
                    )
                    high = item.astype(bf16)
                    highs.append(high)
                    lows.append((item - high.astype(f32)).astype(bf16))
            high, low = jnp.concatenate(highs, axis=1), jnp.concatenate(lows, axis=1)
            value = (
                jnp.dot(tables_ref[2], high, preferred_element_type=f32)
                + jnp.dot(tables_ref[2], low, preferred_element_type=f32)
                + jnp.dot(tables_ref[3], high, preferred_element_type=f32)
            )
            for i, column in enumerate(columns):
                signal[0 : 2 * half, column] = value[:, 2 * i * block : 2 * (i + 1) * block]

    for mask in early:
        hand_on(mask)
    for mask in near:
        if mask >= WHOLE:
            passed[mask].wait_recv()
    filter_places(0, NEAR)
    for mask in late:
        hand_on(mask)
        gate_copy[mask].start()
        gate_copy[mask - NEAR // 2].start()
    for first in range(NEAR, COUNT, 2):
        for mask in (first, first + 1):
            passed[mask].wait_recv()
        filter_places(first, 2)
    scale = 1.0 / (2 * COUNT * tokens)

    def gather(step):
        here = pl.ds(pl.multiple_of(step * tile, tile), tile)
        there = pl.ds(pl.multiple_of(half + step * tile, tile), tile)
        sums = None
        for parity in range(2):
            waves = [None] * COUNT
            for place in range(COUNT):
                column = 2 * place + parity
                columns = slice(column * block, (column + 1) * block)
                re, im = signal[here, columns], signal[there, columns]
                cos = twist_ref[here, column : column + 1]
                sin = twist_ref[here, 2 * COUNT + column : 2 * COUNT + column + 1]
                waves[reverse(place)] = (re * cos + im * sin, im * cos - re * sin)
            pairs = short_transform(waves, 1)
            parts = [times_root(pair, source * parity, 2 * COUNT)[0] for source, pair in enumerate(pairs)]
            sums = parts if sums is None else [left + right for left, right in zip(sums, parts)]
        for source in range(COUNT):
            result[source, here, :] = sums[source] * scale

    pl.loop(0, tokens // tile)(gather)

    mirror_copy, owner_copy = {}, {}
    for mask in range(1, COUNT):
        mirror_copy[mask] = remote(
            MIRROR, mask, blocks.at[(mask + NEAR) % COUNT], mirror_rows.at[:, lanes(device)]
        )
        owner_copy[mask] = remote(OWNER, mask, blocks.at[mask], own_rows.at[:, lanes(device)])

    def make_block(mask):
        source = peers[mask]
        blocks[mask] = (result[source] * got_gate[source].astype(f32)).astype(bf16)

    for mask in range(NEAR):
        if mask:
            gate_copy[mask].wait_recv()
        make_block(mask)
        mirror_copy[mask + NEAR].start()
        if mask:
            owner_copy[mask].start()
    own_rows[:, lanes(device)] = blocks[0]
    for mask in range(NEAR):
        gate_copy[mask + NEAR].wait_recv()
        make_block(mask + NEAR)
        if mask:
            mirror_copy[mask].start()
    mirror_rows[:, lanes(device)] = blocks[NEAR]
    for copy in routes:
        copy.wait()

    near_rows = NEAR * HEAD
    columns_of = [
        pl.ds(pl.multiple_of(base * half_channels, half_channels), half_channels)
        for base in (high_bit, 1 - high_bit)
    ]

    def part_of(chunk, part):
        base = (high_bit, 1 - high_bit)[chunk] * half_channels + part * part_width
        return pl.ds(pl.multiple_of(base, part_width), part_width)

    def targets_of(ids, picks):
        position = jnp.full_like(ids, -1024)
        for mask in range(COUNT):
            position = jnp.where(ids == peers[mask], mask * HEAD, position)
        head = jnp.where(picks < HEAD, position + picks, -1024)
        tail = jnp.where((picks >= HEAD) & (picks < CAP), position + picks - HEAD, -1024)
        return head, tail

    slot_row = lax.broadcasted_iota(jnp.int32, (near_rows, tokens), 0)

    def hits(targets, shift):
        return [slot_row == targets[pick : pick + 1, :] + shift for pick in range(2)]

    def one_hot(targets, shift):
        first, second = hits(targets, shift)
        return jnp.where(first | second, 1.0, 0.0).astype(bf16)

    send_copy = {}
    for kind in range(2):
        for chunk in range(2):
            buffer = 2 * kind + chunk
            for mask in range(NEAR):
                span = pl.ds(mask * HEAD, HEAD)
                src, dst = packed.at[buffer, span], arrived.at[buffer, span]
                if mask:
                    send_copy[buffer, mask] = remote(SEND + buffer, mask, src, dst)
                else:
                    send_copy[buffer, mask] = pltpu.make_async_copy(src, dst, own_sem.at[buffer])

    def dispatch(kind, chunk, source, targets):
        head, tail = targets
        buffer = 2 * kind + chunk
        packed[buffer, :, 0:half_channels] = jnp.dot(
            one_hot(head, 0), source[:, columns_of[chunk]], preferred_element_type=f32
        ).astype(bf16)
        tails = jnp.zeros((near_rows, part_width), f32)
        for part in range(PARTS):
            tails = tails + jnp.dot(
                one_hot(tail, TAIL * part), source[:, part_of(chunk, part)], preferred_element_type=f32
            )
        packed[buffer, :, half_channels:] = tails.astype(bf16)
        for mask in reversed(range(NEAR)):
            send_copy[buffer, mask].start()

    mirror_targets = targets_of(mirror_ids[...], mirror_picks[...])
    for mask in near:
        mirror_copy[mask].wait_recv()
    dispatch(0, 0, mirror_rows, mirror_targets)
    own_targets = targets_of(ids_ref[...], picks_ref[...])

    def dispatch_near():
        for mask in near:
            owner_copy[mask].wait_recv()
        dispatch(1, 0, own_rows, own_targets)

    def dispatch_far():
        for mask in far:
            owner_copy[mask].wait_recv()
        dispatch(1, 1, own_rows, own_targets)

    for mask in far:
        mirror_copy[mask].wait_recv()
    dispatch(0, 1, mirror_rows, mirror_targets)
    dispatch_near()
    for mask in far:
        owner_copy[mask].start()

    tail_rows = NEAR * TAIL
    pick_row = lax.broadcasted_iota(jnp.int32, (tail_rows, near_rows), 0)
    pick_col = lax.broadcasted_iota(jnp.int32, (tail_rows, near_rows), 1)
    pick_base = (pick_row // TAIL) * HEAD + pick_row % TAIL

    def selection(part):
        return jnp.where(pick_col == pick_base + TAIL * part, 1.0, 0.0).astype(bf16)

    back_row = lax.broadcasted_iota(jnp.int32, (near_rows, tail_rows), 0)
    back_col = lax.broadcasted_iota(jnp.int32, (near_rows, tail_rows), 1)
    back_base = (back_col // TAIL) * HEAD + back_col % TAIL

    def placing(part):
        return jnp.where(back_row == back_base + TAIL * part, 1.0, 0.0).astype(bf16)

    back_copy = {}
    for chunk in range(BACKS):
        for mask in range(COUNT):
            kind = 0 if mask >= NEAR else 1
            src = done.at[BACKS * kind + chunk, pl.ds(mask % NEAR * HEAD, HEAD)]
            dst = back.at[chunk, pl.ds(mask * HEAD, HEAD)]
            if mask:
                back_copy[chunk, mask] = remote(BACK + chunk, mask, src, dst)
            else:
                back_copy[chunk, mask] = pltpu.make_async_copy(src, dst, own_sem.at[4 + chunk])

    def normalise(source, destination, count):
        @pl.loop(0, count // tile)
        def _(step):
            here = pl.ds(pl.multiple_of(step * tile, tile), tile)
            item = source[here, :].astype(f32)
            mean = jnp.sum(item * item, axis=1, keepdims=True) / channels
            destination[here, :] = (item * lax.rsqrt(mean + 1e-06)).astype(bf16)

    group_rows = near_rows + tail_rows
    wide = 256
    back_width = channels // BACKS
    back_part = back_width // PARTS

    def take(kind, chunk):
        buffer = 2 * kind + chunk
        for mask in range(NEAR):
            if mask:
                send_copy[buffer, mask].wait_recv()
            else:
                send_copy[buffer, mask].wait()
        rows[0:near_rows, columns_of[chunk]] = arrived[buffer, :, 0:half_channels]
        for part in range(PARTS):
            rows[near_rows:group_rows, part_of(chunk, part)] = jnp.dot(
                selection(part), arrived[buffer, :, half_channels:], preferred_element_type=f32
            ).astype(bf16)

    def squares(chunk):
        @pl.loop(0, group_rows // tile)
        def _(step):
            here = pl.ds(pl.multiple_of(step * tile, tile), tile)
            item = rows[here, columns_of[chunk]].astype(f32)
            part = jnp.sum(item * item, axis=1, keepdims=True)
            if chunk == 0:
                inverse[here, :] = jnp.broadcast_to(part, (tile, wide))
            else:
                mean = (inverse[here, :] + part) / channels
                inverse[here, :] = lax.rsqrt(mean + 1e-06)

    def expert(kind):
        take(kind, 0)
        if kind == 0:
            weights[0].wait()
            weights[1].wait()

        @pl.loop(0, hidden_size // wide)
        def _(step):
            columns = pl.ds(pl.multiple_of(step * wide, wide), wide)
            item = rows[:, columns_of[0]]
            signal[0:group_rows, columns] = jnp.dot(
                item, wg[columns_of[0], columns], preferred_element_type=f32
            )
            signal[group_rows : 2 * group_rows, columns] = jnp.dot(
                item, wu[columns_of[0], columns], preferred_element_type=f32
            )

        squares(0)
        take(kind, 1)
        squares(1)

        def pair(step):
            columns = pl.ds(pl.multiple_of(step * wide, wide), wide)
            item = rows[:, columns_of[1]]
            gate_part = signal[0:group_rows, columns] + jnp.dot(
                item, wg[columns_of[1], columns], preferred_element_type=f32
            )
            up_part = signal[group_rows : 2 * group_rows, columns] + jnp.dot(
                item, wu[columns_of[1], columns], preferred_element_type=f32
            )
            return gate_part, up_part

        def keep(slot, parts):
            gate_sum[slot], up_sum[slot] = parts

        def activate(step, slot):
            columns = pl.ds(pl.multiple_of(step * wide, wide), wide)
            scales = inverse[...]
            hidden[:, columns] = (
                jax.nn.silu(gate_sum[slot] * scales) * (up_sum[slot] * scales)
            ).astype(bf16)

        last = hidden_size // wide - 1
        keep(0, pair(0))

        @pl.loop(0, last // 2)
        def _(step):
            for odd in range(2):
                parts = pair(2 * step + odd + 1)
                activate(2 * step + odd, odd)
                keep(1 - odd, parts)

        if last % 2:
            parts = pair(last)
            activate(last - 1, 0)
            keep(1, parts)
        activate(last, last % 2)

        if kind == 0:
            weights[2].wait()
        steps = half_channels * 2 // BACKS // wide
        for chunk in range(BACKS):
            buffer = BACKS * kind + chunk
            tail_sum[...] = jnp.zeros_like(tail_sum)

            @pl.loop(0, steps)
            def _(step):
                inner = pl.ds(pl.multiple_of(step * wide, wide), wide)
                columns = pl.ds(pl.multiple_of((chunk * steps + step) * wide, wide), wide)
                value = jnp.dot(hidden[...], wd[:, columns], preferred_element_type=f32).astype(bf16)
                done[buffer, :, inner] = value[0:near_rows, :]
                tails = tail_sum[...]
                for side in range(wide // back_part):
                    tails = tails + jnp.dot(
                        placing(step * (wide // back_part) + side),
                        value[near_rows:group_rows, side * back_part : (side + 1) * back_part],
                        preferred_element_type=f32,
                    )
                tail_sum[...] = tails

            done[buffer, :, back_width:] = tail_sum[...].astype(bf16)
            for mask in far if kind == 0 else range(NEAR):
                back_copy[chunk, mask].start()
            if kind == 0 and chunk == BACKS // 2 - 1:
                dispatch_far()

    expert(0)
    normalise(own_rows, normed, tokens)
    logits = lax.dot_general(
        router_ref[...], normed[...], (((1,), (1,)), ((), ())), preferred_element_type=f32
    )
    expert_row = lax.broadcasted_iota(jnp.int32, logits.shape, 0)
    for pick in range(2):
        chosen = jnp.sum(
            jnp.where(expert_row == ids_ref[pick : pick + 1, :], logits, 0.0), axis=0, keepdims=True
        )
        gates[pick : pick + 1, :] = jax.nn.sigmoid(chosen)
    expert(1)

    def weights_of(targets, shift):
        first, second = hits(targets, shift)
        mix = jnp.where(first, gates[0:1, :], 0.0) + jnp.where(second, gates[1:2, :], 0.0)
        mix = mix.T
        high = mix.astype(bf16)
        return high, (mix - high.astype(f32)).astype(bf16)

    def weighted(pair, values):
        return sum(jnp.dot(piece, values, preferred_element_type=f32) for piece in pair)

    head, tail = own_targets
    for side in range(2):
        shift = -side * near_rows
        span = slice(side * near_rows, (side + 1) * near_rows)
        head_pair = weights_of(head, shift)
        tail_pairs = [weights_of(tail, shift + TAIL * part) for part in range(PARTS)]
        for chunk in range(BACKS):
            for mask in range(side * NEAR, (side + 1) * NEAR):
                if mask:
                    back_copy[chunk, mask].wait_recv()
                else:
                    back_copy[chunk, mask].wait()
            columns = slice(chunk * back_width, (chunk + 1) * back_width)
            added = weighted(head_pair, back[chunk, span, 0:back_width]) + jnp.concatenate(
                [weighted(pair, back[chunk, span, back_width:]) for pair in tail_pairs], axis=1
            )
            if side == 0:
                total[:, columns] = own_rows[:, columns].astype(f32) + added
            else:
                out_ref[:, columns] = (total[:, columns] + added).astype(bf16)

    for mask in range(1, COUNT):
        values_copy[mask].wait_send()
        filter_copy[mask].wait_send()
        gate_copy[mask].wait_send()
        mirror_copy[mask].wait_send()
        owner_copy[mask].wait_send()
        if mask >= WHOLE:
            passed[mask].wait_send()
        for chunk in range(BACKS):
            back_copy[chunk, mask].wait_send()
    for buffer in range(4):
        for mask in near:
            send_copy[buffer, mask].wait_send()
    for mask in far:
        if mask % 2 == 0:
            fold_copy[mask].wait_send()

    @pl.when(device < 2)
    def _():
        for mask in far:
            if mask % 2:
                fold_copy[mask].wait_send()

    @pl.when(paired)
    def _():
        for copy in pair_copy:
            copy.wait_send()


def run_layer(
    value_stream, gate_stream, filter_spectrum, router, w_gate, w_up, w_down, route_ids, route_slots
):
    tokens, channels = value_stream.shape
    hidden_size = w_gate.shape[1]
    block = channels // COUNT
    near_rows = NEAR * HEAD
    half_rows = near_rows + NEAR * TAIL
    part_width = channels // 2 // PARTS
    packed_width = channels // 2 + part_width
    back_width = channels // BACKS + channels // BACKS // PARTS
    vmem = pl.BlockSpec(memory_space=pltpu.VMEM)
    hbm = pl.BlockSpec(memory_space=pl.ANY)
    bf16, f32, i32 = jnp.bfloat16, jnp.float32, jnp.int32
    return pl.pallas_call(
        layer_kernel,
        out_shape=jax.ShapeDtypeStruct((tokens, channels), bf16),
        in_specs=[hbm] * 5 + [vmem] * 3 + [hbm] * 3,
        out_specs=vmem,
        scratch_shapes=[
            pltpu.VMEM((4, 2 * tokens, 2 * tokens), bf16),
            pltpu.VMEM((tokens, 4 * COUNT), f32),
            pltpu.VMEM((COUNT, tokens, block), bf16),
            pltpu.VMEM((2, 2, COUNT, tokens, block), bf16),
            pltpu.VMEM((COUNT, tokens, block), bf16),
            pltpu.VMEM((NEAR // 2, tokens, block), bf16),
            pltpu.VMEM((NEAR // 2, tokens, block), bf16),
            pltpu.VMEM((NEAR // 2, tokens, block), bf16),
            pltpu.VMEM((2 * tokens, 2 * channels), bf16),
            pltpu.VMEM((2 * tokens, 2 * channels), bf16),
            pltpu.VMEM((max(2 * tokens, 2 * half_rows), 2 * channels), f32),
            pltpu.VMEM((COUNT, tokens, block), f32),
            pltpu.VMEM((COUNT, tokens, block), bf16),
            pltpu.VMEM((tokens, channels), bf16),
            pltpu.VMEM((tokens, channels), bf16),
            pltpu.VMEM((tokens, channels), bf16),
            pltpu.VMEM((2, tokens), i32),
            pltpu.VMEM((2, tokens), i32),
            pltpu.VMEM((4, near_rows, packed_width), bf16),
            pltpu.VMEM((4, near_rows, packed_width), bf16),
            pltpu.VMEM((half_rows, channels), bf16),
            pltpu.VMEM((half_rows, hidden_size), bf16),
            pltpu.VMEM((channels, hidden_size), bf16),
            pltpu.VMEM((channels, hidden_size), bf16),
            pltpu.VMEM((hidden_size, channels), bf16),
            pltpu.VMEM((half_rows, 256), f32),
            pltpu.VMEM((2, half_rows, 256), f32),
            pltpu.VMEM((2, half_rows, 256), f32),
            pltpu.VMEM((2 * BACKS, near_rows, back_width), bf16),
            pltpu.VMEM((BACKS, 2 * near_rows, back_width), bf16),
            pltpu.VMEM((near_rows, channels // BACKS // PARTS), f32),
            pltpu.VMEM((8, tokens), f32),
            pltpu.VMEM((tokens, channels), f32),
            pltpu.SemaphoreType.DMA((4 + BACKS,)),
            pltpu.SemaphoreType.DMA((KINDS, COUNT)),
            pltpu.SemaphoreType.DMA((KINDS, COUNT)),
            pltpu.SemaphoreType.DMA((3,)),
            pltpu.SemaphoreType.DMA((NEAR // 2,)),
        ],
        compiler_params=pltpu.CompilerParams(
            collective_id=1, has_side_effects=True, vmem_limit_bytes=63 * 1024 * 1024
        ),
    )(
        value_stream, gate_stream, filter_spectrum, inner_tables(tokens), twist_table(COUNT, tokens),
        router.T, route_ids, route_slots, w_gate, w_up, w_down,
    )


def local(
    value_stream, gate_stream, filter_spectrum, router, w_gate, w_up, w_down, route_ids, route_slots
):
    tok_rows, channels = value_stream.shape
    size_ctx = lax.axis_size("ctx")
    block = channels // size_ctx
    expert_count = router.shape[1]
    if (
        size_ctx == expert_count == COUNT
        and lax.axis_size("groups") == 2
        and block == tok_rows == 128
        and w_gate.shape[1] % 256 == 0
    ):
        return run_layer(
            value_stream, gate_stream, filter_spectrum, router, w_gate, w_up, w_down, route_ids, route_slots
        )
    arrived = lax.all_to_all(value_stream, "ctx", split_axis=1, concat_axis=0, tiled=True)
    filter_all = lax.all_to_all(filter_spectrum, "ctx", split_axis=3, concat_axis=2, tiled=True)
    long_conv = convolve(arrived, filter_all, size_ctx, tok_rows, block)
    long_conv = lax.all_to_all(
        long_conv.astype(jnp.bfloat16), "ctx", split_axis=0, concat_axis=1, tiled=True
    )
    long_conv = long_conv.astype(jnp.float32)
    hyena_out = (gate_stream.astype(jnp.float32) * long_conv).astype(jnp.bfloat16)
    hyena32 = hyena_out.astype(jnp.float32)
    inv_rms = lax.rsqrt(jnp.mean(hyena32 * hyena32, axis=1, keepdims=True) + 1e-06)
    normed = (hyena32 * inv_rms).astype(jnp.bfloat16)
    logits = jnp.dot(normed, router, preferred_element_type=jnp.float32)
    owner_split = size_ctx // expert_count
    slot_count = expert_count * CAP
    positions = jnp.arange(slot_count, dtype=jnp.int32)
    expert_range = jnp.arange(expert_count, dtype=jnp.int32)
    combine = jnp.zeros((tok_rows, slot_count), jnp.float32)
    dispatch = jnp.zeros((slot_count, channels), jnp.float32)
    for pick_index in range(route_ids.shape[0]):
        expert_ids = route_ids[pick_index]
        slot_ids = route_slots[pick_index]
        target = jnp.where(slot_ids < CAP, expert_ids * CAP + slot_ids, -1)
        slot_hits = target[:, None] == positions[None, :]
        chosen_logit = jnp.sum(
            jnp.where(expert_ids[:, None] == expert_range[None, :], logits, 0.0), axis=1
        )
        gate_value = jax.nn.sigmoid(chosen_logit)
        combine = combine + slot_hits.astype(jnp.float32) * gate_value[:, None]
        dispatch = dispatch + lax.dot_general(
            slot_hits.astype(jnp.bfloat16),
            normed,
            (((0,), (0,)), ((), ())),
            preferred_element_type=jnp.float32,
        )
    buffer = dispatch.astype(jnp.bfloat16).reshape(expert_count, CAP, channels)
    outgoing = jnp.repeat(buffer, owner_split, axis=0)
    slot_rows = lax.all_to_all(outgoing, "ctx", split_axis=0, concat_axis=0, tiled=True)
    flat_rows = slot_rows.reshape(-1, channels)
    gate_part = jnp.dot(flat_rows, w_gate, preferred_element_type=jnp.float32)
    up_part = jnp.dot(flat_rows, w_up, preferred_element_type=jnp.float32)
    hidden = (jax.nn.silu(gate_part) * up_part).astype(jnp.bfloat16)
    partial_value = jnp.dot(hidden, w_down, preferred_element_type=jnp.float32).astype(jnp.bfloat16)
    returned = lax.all_to_all(
        partial_value.reshape(slot_rows.shape), "ctx", split_axis=0, concat_axis=0, tiled=True
    )
    expert_out = jnp.sum(
        returned.astype(jnp.float32).reshape(expert_count, owner_split, CAP, channels), axis=1
    ).reshape(slot_count, channels)
    contribution = jnp.dot(combine, expert_out, precision=highest)
    return (hyena32 + contribution).astype(jnp.bfloat16)


def solution(mesh):
    in_specs = (
        P(("groups", "ctx"), None),
        P(("groups", "ctx"), None),
        P(None, None, "ctx", None),
        P(),
        P(None, "ctx"),
        P(None, "ctx"),
        P("ctx", None),
        P(None, ("groups", "ctx")),
        P(None, ("groups", "ctx")),
    )
    out_specs = P(("groups", "ctx"), None)
    return jax.shard_map(local, mesh=mesh, in_specs=in_specs, out_specs=out_specs, check_vma=False)
```

```python
import jax
import jax.numpy as jnp
import numpy as np
from jax import lax
from jax.experimental import pallas as pl
from jax.experimental.pallas import tpu as pltpu
from jax.sharding import PartitionSpec as P

CAP = 20


two_pi = 2.0 * np.pi
highest = lax.Precision.HIGHEST


def reverse_bits(length_n):
    bit_count = length_n.bit_length() - 1
    positions = np.arange(length_n)
    reversed_index = np.zeros(length_n, dtype=np.int64)
    for position in range(bit_count):
        reversed_index = reversed_index | (positions >> position & 1) << bit_count - 1 - position
    return reversed_index


def spread_table(size_ctx):
    rho = 2 * reverse_bits(size_ctx)[None, :] + np.arange(2)[:, None]
    angle_rad = -two_pi * (np.outer(rho.reshape(-1), np.arange(size_ctx)) % (2 * size_ctx)) / (2 * size_ctx)
    parts = np.stack([np.cos(angle_rad), np.sin(angle_rad)], axis=1)
    return jnp.asarray(parts, jnp.float32)


def fine_table(size_ctx, tok_rows):
    total = 2 * size_ctx * tok_rows
    rho = (2 * reverse_bits(size_ctx)[None, :] + np.arange(2)[:, None]).reshape(-1)
    k = 2 * size_ctx * reverse_bits(tok_rows)[None, :] + rho[:, None]
    step = (k[:, :, None] * np.arange(tok_rows)[None, None, :]) % total
    angle_rad = -two_pi * step / total
    re, im = np.cos(angle_rad), np.sin(angle_rad)
    table = np.stack([np.stack([re, -im], axis=2), np.stack([im, re], axis=2)], axis=1)
    return jnp.asarray(table.reshape(2 * size_ctx, 2 * tok_rows, 2 * tok_rows), jnp.float32)


def convolve(arrived, filter_all, size_ctx, tok_rows, block):
    rho_count = 2 * size_ctx
    coarse = spread_table(size_ctx)
    fine = fine_table(size_ctx, tok_rows)
    samples = arrived.astype(jnp.float32).reshape(size_ctx, tok_rows * block)
    spread = jnp.dot(coarse.reshape(2 * rho_count, size_ctx), samples, precision=highest)
    spread = spread.reshape(rho_count, 2 * tok_rows, block)
    signal = jnp.einsum("rqt,rtc->rqc", fine, spread, precision=highest)
    signal = signal.reshape(rho_count, 2, tok_rows, block)
    filter32 = filter_all.astype(jnp.float32).reshape(2, rho_count, tok_rows, block)
    real_part = signal[:, 0] * filter32[0] - signal[:, 1] * filter32[1]
    imag_part = signal[:, 0] * filter32[1] + signal[:, 1] * filter32[0]
    signal = jnp.concatenate([real_part, imag_part], axis=1)
    spread = jnp.einsum("rqt,rqc->rtc", fine, signal, precision=highest)
    spread = spread.reshape(2 * rho_count, tok_rows * block)
    folded = jnp.dot(coarse.reshape(2 * rho_count, size_ctx).T, spread, precision=highest)
    return (folded / (rho_count * tok_rows)).reshape(size_ctx * tok_rows, block)


def flip_bits(index, mask):
    result = index
    bit = 1
    while bit <= mask:
        if mask & bit:
            result = result + bit * (1 - 2 * ((index // bit) % 2))
        bit *= 2
    return result


COUNT = 16
NEAR = COUNT // 2
HEAD = 16
TAIL = CAP - HEAD
PARTS = HEAD // TAIL


def twist_table(size_ctx, tok_rows):
    rho = (2 * reverse_bits(size_ctx)[:, None] + np.arange(2)[None, :]).reshape(-1)
    angle_rad = -two_pi * np.outer(np.arange(tok_rows), rho) / (2 * size_ctx * tok_rows)
    return jnp.asarray(np.concatenate([np.cos(angle_rad), np.sin(angle_rad)], axis=1), jnp.float32)


def inner_tables(tok_rows):
    angle_rad = -two_pi * (np.outer(reverse_bits(tok_rows), np.arange(tok_rows)) % tok_rows) / tok_rows
    re, im = np.cos(angle_rad), np.sin(angle_rad)
    table = np.block([[re, -im], [im, re]]).astype(np.float32)
    pieces = []
    for matrix in (table, table.T):
        high = matrix.astype(jnp.bfloat16)
        low = (matrix - high.astype(np.float32)).astype(jnp.bfloat16)
        pieces += [high, low]
    return jnp.asarray(np.stack(pieces))


def times_root(pair, power, order):
    power %= order
    re, im = pair
    if power == 0:
        return pair
    if im is None and 4 * power % order:
        cos, sin = float(np.cos(two_pi * power / order)), float(np.sin(two_pi * power / order))
        return (re * cos, re * sin)
    if im is None:
        im = jnp.zeros_like(re)
    if 4 * power == order:
        return (-im, re)
    if 2 * power == order:
        return (-re, -im)
    if 4 * power == 3 * order:
        return (im, -re)
    cos, sin = float(np.cos(two_pi * power / order)), float(np.sin(two_pi * power / order))
    return (re * cos - im * sin, re * sin + im * cos)


def short_transform(values, sign):
    order = len(values)
    if order == 1:
        return values
    even = short_transform(values[0::2], sign)
    odd = short_transform(values[1::2], sign)
    turned = [times_root(odd[i], sign * i, order) for i in range(order // 2)]
    return [(even[i][0] + turned[i][0], even[i][1] + turned[i][1]) for i in range(order // 2)] + [
        (even[i][0] - turned[i][0], even[i][1] - turned[i][1]) for i in range(order // 2)
    ]


VALUES, FILTER, GATE, MIRROR, OWNER, SEND, BACK, ROUTE, PASS, PAIR, FOLD = 0, 1, 2, 3, 4, 5, 9, 13, 14, 15, 16
KINDS = 17
BACKS = 4
WHOLE = 4
EARLY = 2
TURN = 0


def layer_kernel(
    values_hbm, stream_hbm, filter_hbm, tables_hbm, twist_hbm, router_ref, ids_ref, picks_ref, wg_hbm, wu_hbm, wd_hbm,
    out_ref,
    tables_ref, twist_ref, got_values, got_filter, got_gate, pair_rows, own_pair, folded, wave_high, wave_low, signal, result, blocks,
    own_rows, mirror_rows, normed, mirror_ids, mirror_picks, packed, arrived, rows, hidden, wg, wu, wd,
    inverse, gate_sum, up_sum, done, back, tail_sum, gates, total, own_sem, send_sem, recv_sem, weight_sem, pair_sem,
):
    device = lax.axis_index("ctx")
    group = lax.axis_index("groups")
    tokens, channels = own_rows.shape
    block = channels // COUNT
    half_channels = channels // 2
    part_width = half_channels // PARTS
    hidden_size = wg.shape[1]
    bf16, f32 = jnp.bfloat16, jnp.float32
    peers = [flip_bits(device, mask) for mask in range(COUNT)]
    high_bit = device // NEAR
    far = range(NEAR, COUNT)
    near = range(1, NEAR)

    barrier = pltpu.get_barrier_semaphore()
    for mask in range(1, COUNT):
        pl.semaphore_signal(
            barrier, inc=1, device_id={"ctx": peers[mask]}, device_id_type=pl.DeviceIdType.MESH
        )
    pl.semaphore_signal(
        barrier, inc=1, device_id={"groups": 1 - group}, device_id_type=pl.DeviceIdType.MESH
    )

    def lanes(index):
        return pl.ds(pl.multiple_of(index * block, block), block)

    def remote(kind, mask, src, dst, slot=None):
        slot = mask if slot is None else slot
        return pltpu.make_async_remote_copy(
            src_ref=src,
            dst_ref=dst,
            send_sem=send_sem.at[kind, slot],
            recv_sem=recv_sem.at[kind, slot],
            device_id={"ctx": peers[mask]},
            device_id_type=pl.DeviceIdType.MESH,
        )

    own = [
        pltpu.make_async_copy(values_hbm.at[:, lanes(device)], got_values.at[device], own_sem.at[0]),
        pltpu.make_async_copy(
            filter_hbm.at[:, :, :, lanes(device)], got_filter.at[:, :, device], own_sem.at[1]
        ),
        pltpu.make_async_copy(stream_hbm.at[:, lanes(device)], got_gate.at[device], own_sem.at[2]),
        pltpu.make_async_copy(tables_hbm, tables_ref, own_sem.at[3]),
        pltpu.make_async_copy(twist_hbm, twist_ref, own_sem.at[4]),
    ]
    weights = [
        pltpu.make_async_copy(src, dst, weight_sem.at[i])
        for i, (src, dst) in enumerate(((wg_hbm, wg), (wu_hbm, wu), (wd_hbm, wd)))
    ]
    for copy in own:
        copy.start()

    values_copy, filter_copy, gate_copy, passed = {}, {}, {}, {}
    for mask in range(1, COUNT):
        values_copy[mask] = remote(
            VALUES, mask, values_hbm.at[:, lanes(peers[mask])], got_values.at[device]
        )
        gate_copy[mask] = remote(
            GATE, mask, stream_hbm.at[:, lanes(peers[mask])], got_gate.at[device]
        )
        if mask < WHOLE:
            filter_copy[mask] = remote(
                FILTER, mask, filter_hbm.at[:, :, :, lanes(peers[mask])], got_filter.at[:, :, device]
            )
        else:
            filter_copy[mask] = remote(
                FILTER, mask, filter_hbm.at[:, group, :, lanes(peers[mask])], got_filter.at[:, group, device]
            ) if mask < NEAR else remote(
                FILTER, mask, filter_hbm.at[group, 1, :, lanes(peers[mask])], got_filter.at[group, 1, device]
            )
            slab = got_filter.at[:, group, peers[mask]] if mask < NEAR else got_filter.at[group, :, peers[mask]]
            passed[mask] = pltpu.make_async_remote_copy(
                src_ref=slab,
                dst_ref=slab,
                send_sem=send_sem.at[PASS, mask],
                recv_sem=recv_sem.at[PASS, mask],
                device_id={"groups": 1 - group},
                device_id_type=pl.DeviceIdType.MESH,
            )
    core, level, line = device % 2, device // 4 % 2, device // 2 % 2
    partner_mask = high_bit * 7 + (1 - high_bit) * (level * 3 + (1 - level) * line)
    partner = 0
    for bit in (1, 2, 4):
        partner = partner + bit * ((device // bit + partner_mask // bit) % 2)
    partner = partner + NEAR * high_bit
    paired = device >= 2
    quarters = NEAR // 2
    pair_copy, own_pair_copy, fold_copy = [], [], {}
    for quarter in range(quarters):
        base = (1 - high_bit) * NEAR + 2 * quarter
        pair_copy.append(pltpu.make_async_remote_copy(
            src_ref=filter_hbm.at[group, 0, :, lanes(base + 1 - core)],
            dst_ref=pair_rows.at[quarter],
            send_sem=send_sem.at[PAIR, quarter],
            recv_sem=recv_sem.at[PAIR, quarter],
            device_id={"ctx": partner},
            device_id_type=pl.DeviceIdType.MESH,
        ))
        own_pair_copy.append(pltpu.make_async_copy(
            filter_hbm.at[group, 0, :, lanes(base + core)], own_pair.at[quarter], pair_sem.at[quarter]
        ))
    for mask in far:
        source = (
            filter_hbm.at[group, 0, :, lanes(peers[mask])] if mask % 2 else folded.at[peers[mask] // 2 % quarters]
        )
        fold_copy[mask] = remote(FOLD, mask, source, got_filter.at[group, 0, device])
    routes = [
        remote(ROUTE, NEAR, ids_ref, mirror_ids, 0),
        remote(ROUTE, NEAR, picks_ref, mirror_picks, 1),
    ]

    pl.semaphore_wait(barrier, COUNT)
    for mask in far:
        values_copy[mask].start()
        if mask > NEAR:
            values_copy[mask - NEAR].start()
    early = range(NEAR, NEAR + NEAR // 2)
    late = range(NEAR + NEAR // 2, COUNT)
    for copy in own_pair_copy:
        copy.start()

    @pl.when(paired)
    def _():
        for copy in pair_copy:
            copy.start()

    @pl.when(device < 2)
    def _():
        for mask in far:
            if mask % 2:
                fold_copy[mask].start()
        pair_rows[...] = jnp.zeros_like(pair_rows)

    for mask in (*early, *near):
        filter_copy[mask].start()
    for copy in routes:
        copy.start()
    for copy in weights:
        copy.start()
    for copy in own_pair_copy:
        copy.wait()

    @pl.when(paired)
    def _():
        for copy in pair_copy:
            copy.wait_recv()

    sign = (1 - 2 * group).astype(f32)
    flip_row = lax.broadcasted_iota(jnp.int32, (tokens, tokens), 0)
    flip_col = lax.broadcasted_iota(jnp.int32, (tokens, tokens), 1)
    flip = jnp.where(flip_row + flip_col == tokens - 1, 1.0, 0.0).astype(bf16)
    for quarter in range(quarters):
        turned = jnp.dot(flip, pair_rows[quarter], preferred_element_type=f32)
        folded[quarter] = (own_pair[quarter].astype(f32) + sign * turned).astype(bf16)
    for mask in far:
        if mask % 2 == 0:
            fold_copy[mask].start()
    for mask in (*near, *far):
        values_copy[mask].wait_recv()
    for mask in late:
        filter_copy[mask].start()
    for mask in near:
        gate_copy[mask].start()
    for copy in own:
        copy.wait()

    def reverse(index):
        return int(reverse_bits(COUNT)[index])

    half = tokens
    tile = 16

    def spread(step):
        here = pl.ds(pl.multiple_of(step * tile, tile), tile)
        there = pl.ds(pl.multiple_of(half + step * tile, tile), tile)
        samples = [got_values[source, here, :].astype(f32) for source in range(COUNT)]
        zero = jnp.zeros_like(samples[0])
        for parity in range(2):
            pairs = [
                times_root((item, None), -source * parity, 2 * COUNT)
                for source, item in enumerate(samples)
            ]
            pairs = [(re, zero if im is None else im) for re, im in pairs]
            waves = short_transform(pairs, -1)
            for place in range(COUNT):
                re, im = waves[reverse(place)]
                column = 2 * place + parity
                cos = twist_ref[here, column : column + 1]
                sin = twist_ref[here, 2 * COUNT + column : 2 * COUNT + column + 1]
                for span, item in ((here, re * cos - im * sin), (there, re * sin + im * cos)):
                    high = item.astype(bf16)
                    columns = slice(column * block, (column + 1) * block)
                    wave_high[span, columns] = high
                    wave_low[span, columns] = (item - high.astype(f32)).astype(bf16)

    def hand_on(mask):
        filter_copy[mask].wait_recv()
        if mask >= NEAR and mask % 2 == 0:
            fold_copy[mask].wait_recv()
        if mask >= NEAR and mask % 2:
            @pl.when(peers[mask] < 2)
            def _():
                fold_copy[mask].wait_recv()

            @pl.when(peers[mask] >= 2)
            def _():
                got_filter[group, 0, peers[mask]] = jnp.zeros((tokens, block), bf16)

        if mask >= WHOLE:
            passed[mask].start()

    pl.loop(0, tokens // tile // 2)(spread)
    for mask in near:
        hand_on(mask)
    pl.loop(tokens // tile // 2, tokens // tile)(spread)

    def product(which, columns):
        high, low = wave_high[:, columns], wave_low[:, columns]
        return (
            jnp.dot(tables_ref[which], high, preferred_element_type=f32)
            + jnp.dot(tables_ref[which], low, preferred_element_type=f32)
            + jnp.dot(tables_ref[which + 1], high, preferred_element_type=f32)
        )

    width = 4 * block

    @pl.loop(0, 2 * channels // width)
    def _(step):
        columns = pl.ds(pl.multiple_of(step * width, width), width)
        signal[0 : 2 * half, columns] = product(0, columns)

    def filter_places(first, number):
        @pl.loop(0, number // 2)
        def _(step):
            columns, highs, lows = [], [], []
            for mask in (first + 2 * step, first + 2 * step + 1):
                place = 0
                for bit in (1, 2, 4, 8):
                    place = place + bit * ((device // bit + mask // bit) % 2)
                columns.append(pl.ds(pl.multiple_of(2 * place * block, 2 * block), 2 * block))
                for parity in range(2):
                    lane = pl.ds(pl.multiple_of((2 * place + parity) * block, block), block)
                    re, im = signal[0:half, lane], signal[half : 2 * half, lane]
                    filter_re = got_filter[0, parity, place].astype(f32)
                    filter_im = got_filter[1, parity, place].astype(f32)
                    item = jnp.concatenate(
                        [re * filter_re - im * filter_im, re * filter_im + im * filter_re], axis=0
                    )
                    high = item.astype(bf16)
                    highs.append(high)
                    lows.append((item - high.astype(f32)).astype(bf16))
            high, low = jnp.concatenate(highs, axis=1), jnp.concatenate(lows, axis=1)
            value = (
                jnp.dot(tables_ref[2], high, preferred_element_type=f32)
                + jnp.dot(tables_ref[2], low, preferred_element_type=f32)
                + jnp.dot(tables_ref[3], high, preferred_element_type=f32)
            )
            for i, column in enumerate(columns):
                signal[0 : 2 * half, column] = value[:, 2 * i * block : 2 * (i + 1) * block]

    for mask in early:
        hand_on(mask)
    for mask in near:
        if mask >= WHOLE:
            passed[mask].wait_recv()
    filter_places(0, NEAR)
    for mask in late:
        hand_on(mask)
        gate_copy[mask].start()
        gate_copy[mask - NEAR // 2].start()
    for first in range(NEAR, COUNT, 2):
        for mask in (first, first + 1):
            passed[mask].wait_recv()
        filter_places(first, 2)
    scale = 1.0 / (2 * COUNT * tokens)

    def gather(step):
        here = pl.ds(pl.multiple_of(step * tile, tile), tile)
        there = pl.ds(pl.multiple_of(half + step * tile, tile), tile)
        sums = None
        for parity in range(2):
            waves = [None] * COUNT
            for place in range(COUNT):
                column = 2 * place + parity
                columns = slice(column * block, (column + 1) * block)
                re, im = signal[here, columns], signal[there, columns]
                cos = twist_ref[here, column : column + 1]
                sin = twist_ref[here, 2 * COUNT + column : 2 * COUNT + column + 1]
                waves[reverse(place)] = (re * cos + im * sin, im * cos - re * sin)
            pairs = short_transform(waves, 1)
            parts = [times_root(pair, source * parity, 2 * COUNT)[0] for source, pair in enumerate(pairs)]
            sums = parts if sums is None else [left + right for left, right in zip(sums, parts)]
        for source in range(COUNT):
            result[source, here, :] = sums[source] * scale

    pl.loop(0, tokens // tile)(gather)

    mirror_copy, owner_copy = {}, {}
    for mask in range(1, COUNT):
        mirror_copy[mask] = remote(
            MIRROR, mask, blocks.at[(mask + NEAR) % COUNT], mirror_rows.at[:, lanes(device)]
        )
        owner_copy[mask] = remote(OWNER, mask, blocks.at[mask], own_rows.at[:, lanes(device)])

    def make_block(mask):
        source = peers[mask]
        blocks[mask] = (result[source] * got_gate[source].astype(f32)).astype(bf16)

    for mask in range(NEAR):
        if mask:
            gate_copy[mask].wait_recv()
        make_block(mask)
        mirror_copy[mask + NEAR].start()
        if mask:
            owner_copy[mask].start()
    own_rows[:, lanes(device)] = blocks[0]
    for mask in range(NEAR):
        gate_copy[mask + NEAR].wait_recv()
        make_block(mask + NEAR)
        if mask:
            mirror_copy[mask].start()
    mirror_rows[:, lanes(device)] = blocks[NEAR]
    for copy in routes:
        copy.wait()

    near_rows = NEAR * HEAD
    columns_of = [
        pl.ds(pl.multiple_of(base * half_channels, half_channels), half_channels)
        for base in (high_bit, 1 - high_bit)
    ]

    def part_of(chunk, part):
        base = (high_bit, 1 - high_bit)[chunk] * half_channels + part * part_width
        return pl.ds(pl.multiple_of(base, part_width), part_width)

    def targets_of(ids, picks):
        position = jnp.full_like(ids, -1024)
        for mask in range(COUNT):
            position = jnp.where(ids == peers[mask], mask * HEAD, position)
        head = jnp.where(picks < HEAD, position + picks, -1024)
        tail = jnp.where((picks >= HEAD) & (picks < CAP), position + picks - HEAD, -1024)
        return head, tail

    slot_row = lax.broadcasted_iota(jnp.int32, (near_rows, tokens), 0)

    def hits(targets, shift):
        return [slot_row == targets[pick : pick + 1, :] + shift for pick in range(2)]

    def one_hot(targets, shift):
        first, second = hits(targets, shift)
        return jnp.where(first | second, 1.0, 0.0).astype(bf16)

    send_copy = {}
    for kind in range(2):
        for chunk in range(2):
            buffer = 2 * kind + chunk
            for mask in range(NEAR):
                span = pl.ds(mask * HEAD, HEAD)
                src, dst = packed.at[buffer, span], arrived.at[buffer, span]
                if mask:
                    send_copy[buffer, mask] = remote(SEND + buffer, mask, src, dst)
                else:
                    send_copy[buffer, mask] = pltpu.make_async_copy(src, dst, own_sem.at[buffer])

    def dispatch(kind, chunk, source, targets):
        head, tail = targets
        buffer = 2 * kind + chunk
        packed[buffer, :, 0:half_channels] = jnp.dot(
            one_hot(head, 0), source[:, columns_of[chunk]], preferred_element_type=f32
        ).astype(bf16)
        tails = jnp.zeros((near_rows, part_width), f32)
        for part in range(PARTS):
            tails = tails + jnp.dot(
                one_hot(tail, TAIL * part), source[:, part_of(chunk, part)], preferred_element_type=f32
            )
        packed[buffer, :, half_channels:] = tails.astype(bf16)
        for mask in reversed(range(NEAR)):
            send_copy[buffer, mask].start()

    mirror_targets = targets_of(mirror_ids[...], mirror_picks[...])
    for mask in near:
        mirror_copy[mask].wait_recv()
    dispatch(0, 0, mirror_rows, mirror_targets)
    own_targets = targets_of(ids_ref[...], picks_ref[...])

    def dispatch_near():
        for mask in near:
            owner_copy[mask].wait_recv()
        dispatch(1, 0, own_rows, own_targets)

    def dispatch_far():
        for mask in far:
            owner_copy[mask].wait_recv()
        dispatch(1, 1, own_rows, own_targets)

    for mask in far:
        mirror_copy[mask].wait_recv()
    dispatch(0, 1, mirror_rows, mirror_targets)
    dispatch_near()
    for mask in far:
        owner_copy[mask].start()

    tail_rows = NEAR * TAIL
    pick_row = lax.broadcasted_iota(jnp.int32, (tail_rows, near_rows), 0)
    pick_col = lax.broadcasted_iota(jnp.int32, (tail_rows, near_rows), 1)
    pick_base = (pick_row // TAIL) * HEAD + pick_row % TAIL

    def selection(part):
        return jnp.where(pick_col == pick_base + TAIL * part, 1.0, 0.0).astype(bf16)

    back_row = lax.broadcasted_iota(jnp.int32, (near_rows, tail_rows), 0)
    back_col = lax.broadcasted_iota(jnp.int32, (near_rows, tail_rows), 1)
    back_base = (back_col // TAIL) * HEAD + back_col % TAIL

    def placing(part):
        return jnp.where(back_row == back_base + TAIL * part, 1.0, 0.0).astype(bf16)

    back_copy = {}
    for chunk in range(BACKS):
        for mask in range(COUNT):
            kind = 0 if mask >= NEAR else 1
            src = done.at[BACKS * kind + chunk, pl.ds(mask % NEAR * HEAD, HEAD)]
            dst = back.at[chunk, pl.ds(mask * HEAD, HEAD)]
            if mask:
                back_copy[chunk, mask] = remote(BACK + chunk, mask, src, dst)
            else:
                back_copy[chunk, mask] = pltpu.make_async_copy(src, dst, own_sem.at[4 + chunk])

    def normalise(source, destination, count):
        @pl.loop(0, count // tile)
        def _(step):
            here = pl.ds(pl.multiple_of(step * tile, tile), tile)
            item = source[here, :].astype(f32)
            mean = jnp.sum(item * item, axis=1, keepdims=True) / channels
            destination[here, :] = (item * lax.rsqrt(mean + 1e-06)).astype(bf16)

    group_rows = near_rows + tail_rows
    wide = 256
    back_width = channels // BACKS
    back_part = back_width // PARTS

    def take(kind, chunk):
        buffer = 2 * kind + chunk
        for mask in range(NEAR):
            if mask:
                send_copy[buffer, mask].wait_recv()
            else:
                send_copy[buffer, mask].wait()
        rows[0:near_rows, columns_of[chunk]] = arrived[buffer, :, 0:half_channels]
        for part in range(PARTS):
            rows[near_rows:group_rows, part_of(chunk, part)] = jnp.dot(
                selection(part), arrived[buffer, :, half_channels:], preferred_element_type=f32
            ).astype(bf16)

    def squares(chunk):
        @pl.loop(0, group_rows // tile)
        def _(step):
            here = pl.ds(pl.multiple_of(step * tile, tile), tile)
            item = rows[here, columns_of[chunk]].astype(f32)
            part = jnp.sum(item * item, axis=1, keepdims=True)
            if chunk == 0:
                inverse[here, :] = jnp.broadcast_to(part, (tile, wide))
            else:
                mean = (inverse[here, :] + part) / channels
                inverse[here, :] = lax.rsqrt(mean + 1e-06)

    def expert(kind):
        take(kind, 0)
        if kind == 0:
            weights[0].wait()
            weights[1].wait()

        @pl.loop(0, hidden_size // wide)
        def _(step):
            columns = pl.ds(pl.multiple_of(step * wide, wide), wide)
            item = rows[:, columns_of[0]]
            signal[0:group_rows, columns] = jnp.dot(
                item, wg[columns_of[0], columns], preferred_element_type=f32
            )
            signal[group_rows : 2 * group_rows, columns] = jnp.dot(
                item, wu[columns_of[0], columns], preferred_element_type=f32
            )

        squares(0)
        take(kind, 1)
        squares(1)

        def pair(step):
            columns = pl.ds(pl.multiple_of(step * wide, wide), wide)
            item = rows[:, columns_of[1]]
            gate_part = signal[0:group_rows, columns] + jnp.dot(
                item, wg[columns_of[1], columns], preferred_element_type=f32
            )
            up_part = signal[group_rows : 2 * group_rows, columns] + jnp.dot(
                item, wu[columns_of[1], columns], preferred_element_type=f32
            )
            return gate_part, up_part

        def keep(slot, parts):
            gate_sum[slot], up_sum[slot] = parts

        def activate(step, slot):
            columns = pl.ds(pl.multiple_of(step * wide, wide), wide)
            scales = inverse[...]
            hidden[:, columns] = (
                jax.nn.silu(gate_sum[slot] * scales) * (up_sum[slot] * scales)
            ).astype(bf16)

        last = hidden_size // wide - 1
        keep(0, pair(0))

        @pl.loop(0, last // 2)
        def _(step):
            for odd in range(2):
                parts = pair(2 * step + odd + 1)
                activate(2 * step + odd, odd)
                keep(1 - odd, parts)

        if last % 2:
            parts = pair(last)
            activate(last - 1, 0)
            keep(1, parts)
        activate(last, last % 2)

        if kind == 0:
            weights[2].wait()
        steps = half_channels * 2 // BACKS // wide
        for chunk in range(BACKS):
            buffer = BACKS * kind + chunk
            tail_sum[...] = jnp.zeros_like(tail_sum)

            @pl.loop(0, steps)
            def _(step):
                inner = pl.ds(pl.multiple_of(step * wide, wide), wide)
                columns = pl.ds(pl.multiple_of((chunk * steps + step) * wide, wide), wide)
                value = jnp.dot(hidden[...], wd[:, columns], preferred_element_type=f32).astype(bf16)
                done[buffer, :, inner] = value[0:near_rows, :]
                tails = tail_sum[...]
                for side in range(wide // back_part):
                    tails = tails + jnp.dot(
                        placing(step * (wide // back_part) + side),
                        value[near_rows:group_rows, side * back_part : (side + 1) * back_part],
                        preferred_element_type=f32,
                    )
                tail_sum[...] = tails

            done[buffer, :, back_width:] = tail_sum[...].astype(bf16)
            for mask in far if kind == 0 else range(NEAR):
                back_copy[chunk, mask].start()
            if kind == 0 and chunk == TURN:
                dispatch_far()

    expert(0)
    normalise(own_rows, normed, tokens)
    logits = lax.dot_general(
        router_ref[...], normed[...], (((1,), (1,)), ((), ())), preferred_element_type=f32
    )
    expert_row = lax.broadcasted_iota(jnp.int32, logits.shape, 0)
    for pick in range(2):
        chosen = jnp.sum(
            jnp.where(expert_row == ids_ref[pick : pick + 1, :], logits, 0.0), axis=0, keepdims=True
        )
        gates[pick : pick + 1, :] = jax.nn.sigmoid(chosen)
    expert(1)

    def weights_of(targets, shift):
        first, second = hits(targets, shift)
        mix = jnp.where(first, gates[0:1, :], 0.0) + jnp.where(second, gates[1:2, :], 0.0)
        mix = mix.T
        high = mix.astype(bf16)
        return high, (mix - high.astype(f32)).astype(bf16)

    def weighted(pair, values):
        return sum(jnp.dot(piece, values, preferred_element_type=f32) for piece in pair)

    head, tail = own_targets
    pairs_of = []
    for side in range(2):
        shift = -side * near_rows
        pairs_of.append(
            [weights_of(head, shift)] + [weights_of(tail, shift + TAIL * part) for part in range(PARTS)]
        )
    order = [(1, chunk) for chunk in range(EARLY)]
    order += [(0, chunk) for chunk in range(BACKS)]
    order += [(1, chunk) for chunk in range(EARLY, BACKS)]
    begun = set()
    for side, chunk in order:
        span = slice(side * near_rows, (side + 1) * near_rows)
        for mask in range(side * NEAR, (side + 1) * NEAR):
            if mask:
                back_copy[chunk, mask].wait_recv()
            else:
                back_copy[chunk, mask].wait()
        columns = slice(chunk * back_width, (chunk + 1) * back_width)
        head_pair, *tail_pairs = pairs_of[side]
        added = weighted(head_pair, back[chunk, span, 0:back_width]) + jnp.concatenate(
            [weighted(pair, back[chunk, span, back_width:]) for pair in tail_pairs], axis=1
        )
        if chunk in begun:
            out_ref[:, columns] = (total[:, columns] + added).astype(bf16)
        else:
            total[:, columns] = own_rows[:, columns].astype(f32) + added
            begun.add(chunk)

    for mask in range(1, COUNT):
        values_copy[mask].wait_send()
        filter_copy[mask].wait_send()
        gate_copy[mask].wait_send()
        mirror_copy[mask].wait_send()
        owner_copy[mask].wait_send()
        if mask >= WHOLE:
            passed[mask].wait_send()
        for chunk in range(BACKS):
            back_copy[chunk, mask].wait_send()
    for buffer in range(4):
        for mask in near:
            send_copy[buffer, mask].wait_send()
    for mask in far:
        if mask % 2 == 0:
            fold_copy[mask].wait_send()

    @pl.when(device < 2)
    def _():
        for mask in far:
            if mask % 2:
                fold_copy[mask].wait_send()

    @pl.when(paired)
    def _():
        for copy in pair_copy:
            copy.wait_send()


def run_layer(
    value_stream, gate_stream, filter_spectrum, router, w_gate, w_up, w_down, route_ids, route_slots
):
    tokens, channels = value_stream.shape
    hidden_size = w_gate.shape[1]
    block = channels // COUNT
    near_rows = NEAR * HEAD
    half_rows = near_rows + NEAR * TAIL
    part_width = channels // 2 // PARTS
    packed_width = channels // 2 + part_width
    back_width = channels // BACKS + channels // BACKS // PARTS
    vmem = pl.BlockSpec(memory_space=pltpu.VMEM)
    hbm = pl.BlockSpec(memory_space=pl.ANY)
    bf16, f32, i32 = jnp.bfloat16, jnp.float32, jnp.int32
    return pl.pallas_call(
        layer_kernel,
        out_shape=jax.ShapeDtypeStruct((tokens, channels), bf16),
        in_specs=[hbm] * 5 + [vmem] * 3 + [hbm] * 3,
        out_specs=vmem,
        scratch_shapes=[
            pltpu.VMEM((4, 2 * tokens, 2 * tokens), bf16),
            pltpu.VMEM((tokens, 4 * COUNT), f32),
            pltpu.VMEM((COUNT, tokens, block), bf16),
            pltpu.VMEM((2, 2, COUNT, tokens, block), bf16),
            pltpu.VMEM((COUNT, tokens, block), bf16),
            pltpu.VMEM((NEAR // 2, tokens, block), bf16),
            pltpu.VMEM((NEAR // 2, tokens, block), bf16),
            pltpu.VMEM((NEAR // 2, tokens, block), bf16),
            pltpu.VMEM((2 * tokens, 2 * channels), bf16),
            pltpu.VMEM((2 * tokens, 2 * channels), bf16),
            pltpu.VMEM((max(2 * tokens, 2 * half_rows), 2 * channels), f32),
            pltpu.VMEM((COUNT, tokens, block), f32),
            pltpu.VMEM((COUNT, tokens, block), bf16),
            pltpu.VMEM((tokens, channels), bf16),
            pltpu.VMEM((tokens, channels), bf16),
            pltpu.VMEM((tokens, channels), bf16),
            pltpu.VMEM((2, tokens), i32),
            pltpu.VMEM((2, tokens), i32),
            pltpu.VMEM((4, near_rows, packed_width), bf16),
            pltpu.VMEM((4, near_rows, packed_width), bf16),
            pltpu.VMEM((half_rows, channels), bf16),
            pltpu.VMEM((half_rows, hidden_size), bf16),
            pltpu.VMEM((channels, hidden_size), bf16),
            pltpu.VMEM((channels, hidden_size), bf16),
            pltpu.VMEM((hidden_size, channels), bf16),
            pltpu.VMEM((half_rows, 256), f32),
            pltpu.VMEM((2, half_rows, 256), f32),
            pltpu.VMEM((2, half_rows, 256), f32),
            pltpu.VMEM((2 * BACKS, near_rows, back_width), bf16),
            pltpu.VMEM((BACKS, 2 * near_rows, back_width), bf16),
            pltpu.VMEM((near_rows, channels // BACKS // PARTS), f32),
            pltpu.VMEM((8, tokens), f32),
            pltpu.VMEM((tokens, channels), f32),
            pltpu.SemaphoreType.DMA((4 + BACKS,)),
            pltpu.SemaphoreType.DMA((KINDS, COUNT)),
            pltpu.SemaphoreType.DMA((KINDS, COUNT)),
            pltpu.SemaphoreType.DMA((3,)),
            pltpu.SemaphoreType.DMA((NEAR // 2,)),
        ],
        compiler_params=pltpu.CompilerParams(
            collective_id=1, has_side_effects=True, vmem_limit_bytes=63 * 1024 * 1024
        ),
    )(
        value_stream, gate_stream, filter_spectrum, inner_tables(tokens), twist_table(COUNT, tokens),
        router.T, route_ids, route_slots, w_gate, w_up, w_down,
    )


def local(
    value_stream, gate_stream, filter_spectrum, router, w_gate, w_up, w_down, route_ids, route_slots
):
    tok_rows, channels = value_stream.shape
    size_ctx = lax.axis_size("ctx")
    block = channels // size_ctx
    expert_count = router.shape[1]
    if (
        size_ctx == expert_count == COUNT
        and lax.axis_size("groups") == 2
        and block == tok_rows == 128
        and w_gate.shape[1] % 256 == 0
    ):
        return run_layer(
            value_stream, gate_stream, filter_spectrum, router, w_gate, w_up, w_down, route_ids, route_slots
        )
    arrived = lax.all_to_all(value_stream, "ctx", split_axis=1, concat_axis=0, tiled=True)
    filter_all = lax.all_to_all(filter_spectrum, "ctx", split_axis=3, concat_axis=2, tiled=True)
    long_conv = convolve(arrived, filter_all, size_ctx, tok_rows, block)
    long_conv = lax.all_to_all(
        long_conv.astype(jnp.bfloat16), "ctx", split_axis=0, concat_axis=1, tiled=True
    )
    long_conv = long_conv.astype(jnp.float32)
    hyena_out = (gate_stream.astype(jnp.float32) * long_conv).astype(jnp.bfloat16)
    hyena32 = hyena_out.astype(jnp.float32)
    inv_rms = lax.rsqrt(jnp.mean(hyena32 * hyena32, axis=1, keepdims=True) + 1e-06)
    normed = (hyena32 * inv_rms).astype(jnp.bfloat16)
    logits = jnp.dot(normed, router, preferred_element_type=jnp.float32)
    owner_split = size_ctx // expert_count
    slot_count = expert_count * CAP
    positions = jnp.arange(slot_count, dtype=jnp.int32)
    expert_range = jnp.arange(expert_count, dtype=jnp.int32)
    combine = jnp.zeros((tok_rows, slot_count), jnp.float32)
    dispatch = jnp.zeros((slot_count, channels), jnp.float32)
    for pick_index in range(route_ids.shape[0]):
        expert_ids = route_ids[pick_index]
        slot_ids = route_slots[pick_index]
        target = jnp.where(slot_ids < CAP, expert_ids * CAP + slot_ids, -1)
        slot_hits = target[:, None] == positions[None, :]
        chosen_logit = jnp.sum(
            jnp.where(expert_ids[:, None] == expert_range[None, :], logits, 0.0), axis=1
        )
        gate_value = jax.nn.sigmoid(chosen_logit)
        combine = combine + slot_hits.astype(jnp.float32) * gate_value[:, None]
        dispatch = dispatch + lax.dot_general(
            slot_hits.astype(jnp.bfloat16),
            normed,
            (((0,), (0,)), ((), ())),
            preferred_element_type=jnp.float32,
        )
    buffer = dispatch.astype(jnp.bfloat16).reshape(expert_count, CAP, channels)
    outgoing = jnp.repeat(buffer, owner_split, axis=0)
    slot_rows = lax.all_to_all(outgoing, "ctx", split_axis=0, concat_axis=0, tiled=True)
    flat_rows = slot_rows.reshape(-1, channels)
    gate_part = jnp.dot(flat_rows, w_gate, preferred_element_type=jnp.float32)
    up_part = jnp.dot(flat_rows, w_up, preferred_element_type=jnp.float32)
    hidden = (jax.nn.silu(gate_part) * up_part).astype(jnp.bfloat16)
    partial_value = jnp.dot(hidden, w_down, preferred_element_type=jnp.float32).astype(jnp.bfloat16)
    returned = lax.all_to_all(
        partial_value.reshape(slot_rows.shape), "ctx", split_axis=0, concat_axis=0, tiled=True
    )
    expert_out = jnp.sum(
        returned.astype(jnp.float32).reshape(expert_count, owner_split, CAP, channels), axis=1
    ).reshape(slot_count, channels)
    contribution = jnp.dot(combine, expert_out, precision=highest)
    return (hyena32 + contribution).astype(jnp.bfloat16)


def solution(mesh):
    in_specs = (
        P(("groups", "ctx"), None),
        P(("groups", "ctx"), None),
        P(None, None, "ctx", None),
        P(),
        P(None, "ctx"),
        P(None, "ctx"),
        P("ctx", None),
        P(None, ("groups", "ctx")),
        P(None, ("groups", "ctx")),
    )
    out_specs = P(("groups", "ctx"), None)
    return jax.shard_map(local, mesh=mesh, in_specs=in_specs, out_specs=out_specs, check_vma=False)
```
